32 devices in a mesh: hier: 8 (over y, x, core), col: 4 (over z).
Axes of the slice: x: 2, y: 2, z: 4, core: 2. Of those that a mesh axis runs over, the one named last changes fastest.
Arguments:
- densities: float32 [32, 2, 256, 256], P('hier', None, 'col'), may hold values from -6 to 6
- hamiltonian: float32 [256, 256], replicated, may hold values from -0.35355339 to 0.35355339, as said below
- couplings: float32 [2, 256, 256], replicated, may hold values from -0.088388348 to 0.088388348, as said below
- gamma: float32 [2], replicated, may hold values from 0.005 to 0.05
- coeff: float32 [2, 2], replicated, may hold values from -0.5 to 0.5
- node_count: int32 [8], replicated, may hold values from 2 to 4, as said below
Outputs:
- new_densities: float32 [32, 2, 256, 256], P('hier', None, 'col')
The draws below stay inside these ranges and needn't reach their ends.
Inputs may be any that keep to these rules, and one draw needn't show every extreme that they name: `node_count`: at least one index of hier holds 4 nodes; every index holds 2 or more. `hamiltonian`: symmetric. `couplings`: each of the two matrices is symmetric.
All inputs are finite; a program needn't handle non-finite values.
Results may differ from the reference program's by a relative error of at most 0.00012.
Values sent between devices are 32-bit elements; how exact they have to be, the bound alone decides.
A program may use at most 64 MiB of HBM per device.

```python
import math
import jax
import jax.numpy as jnp
from jax import lax

D = 256
NODE_DEV = 4
DEPTH2 = 2
SHARDS = 8
SLOTS = 32


def draw_hamiltonian(key, part):
    base = jax.random.truncated_normal(key, -4.0, 4.0, (D, D), jnp.float32)
    return ((base + base.T) / jnp.sqrt(2.0 * D)).astype(jnp.float32)


def draw_couplings(key, part):
    base = jax.random.truncated_normal(jax.random.fold_in(key, 7), -4.0, 4.0, (2, D, D), jnp.float32)
    return (0.25 * (base + jnp.swapaxes(base, 1, 2)) / jnp.sqrt(2.0 * D)).astype(jnp.float32)


def draw_node_count(key, part):
    key_counts, key_full = jax.random.split(jax.random.fold_in(key, 11))
    counts = jax.random.randint(key_counts, (SHARDS,), NODE_DEV // 2, NODE_DEV + 1)
    full_index = jax.random.randint(key_full, (), 0, SHARDS)
    return jnp.where(jnp.arange(SHARDS) == full_index, NODE_DEV, counts).astype(jnp.int32)


def steps_of(rng, extent, cuts, smallest, largest):
    level = 1.0
    for axis_at, blocks in cuts:
        draws = jax.random.uniform(jax.random.fold_in(jax.random.fold_in(rng, 6), axis_at), (blocks,), jnp.float32, smallest / len(cuts), largest / len(cuts))
        level = level * jnp.repeat(jnp.exp(draws), extent[axis_at] // blocks).reshape((-1,) + (1,) * (len(extent) - 1 - axis_at))
    return level


def normal_values(stream_key, extent, width, limit, cuts=(), held_as=jnp.bfloat16):
    loudness = steps_of(stream_key, extent, cuts, -0.22, 0.18) if cuts else 1.0
    entries = jax.random.normal(stream_key, extent, jnp.float32) * width * loudness
    return jnp.minimum(jnp.maximum(entries, -limit), limit).astype(held_as)


def setup_inputs(seed: int = 0) -> dict:
    seeds = jax.random.split(jax.random.key(seed), 7)
    return {
        "densities": normal_values(seeds[0], (SLOTS, 2, D, D), 1.0, 6.0, ((0, 8), (2, 4)), jnp.float32),
        "hamiltonian": draw_hamiltonian(jax.random.fold_in(seeds[6], 71), 0),
        "couplings": draw_couplings(jax.random.fold_in(seeds[6], 71), 0),
        "gamma": jnp.clip(jnp.exp(jax.random.uniform(seeds[3], (2,), jnp.float32, math.log(0.005), math.log(0.05))), 0.005, 0.05),
        "coeff": jnp.clip(jax.random.uniform(seeds[4], (2, 2), jnp.float32, -0.5, 0.5), -0.5, 0.5),
        "node_count": draw_node_count(jax.random.fold_in(seeds[6], 71), 0),
    }


step_size = 0.2

def hierarchy(node_count, device, slot):
    shards = node_count.shape[0]
    columns = jnp.arange(shards, dtype=jnp.int32)
    counts = node_count.astype(jnp.int32)
    offsets = (jnp.cumsum(counts) - counts).astype(jnp.int32)
    live_total = (jnp.sum(counts).astype(jnp.int32) // DEPTH2 * DEPTH2).astype(jnp.int32)

    def lookup(table, which):
        return lax.optimization_barrier(jnp.sum(jnp.where(which[:, None] == columns[None, :], table[None, :], 0), axis=1)).astype(jnp.int32)
    index = (lookup(offsets, device) + slot).astype(jnp.int32)
    live = (slot < lookup(counts, device)) & (index < live_total)
    first = index // DEPTH2
    second = index % DEPTH2
    targets = (index + DEPTH2, index + 1, index - DEPTH2, index - 1)
    allowed = (live & (index + DEPTH2 < live_total), live & (second + 1 < DEPTH2), live & (first > 0), live & (second > 0))
    found = []
    for target, valid in zip(targets, allowed):
        owner = (lax.optimization_barrier(jnp.sum((offsets[None, :] <= target[:, None]).astype(jnp.int32), axis=1)) - 1).astype(jnp.int32)
        within = (target - lookup(offsets, owner)).astype(jnp.int32)
        found.append((owner, within, valid))
    return (live, first, second, found)

def combine(upward, downward, raise_w, lower_w, real, imag):
    rise = raise_w[:, None, None]
    fall = lower_w[:, None, None]
    part_re = rise * upward[:, 0] + fall * (real * downward[:, 0] - imag * downward[:, 1])
    part_im = rise * upward[:, 1] + fall * (real * downward[:, 1] + imag * downward[:, 0])
    return jnp.stack([part_re, part_im], axis=1)

def mixes(linked, levels, coeff, sign):
    result = []
    for mode in range(2):
        result.append(combine(linked[mode], linked[mode + 2], jnp.sqrt(levels[mode] + 1.0), jnp.sqrt(levels[mode]), coeff[mode, 0], sign * coeff[mode, 1]))
    return result

def reference(densities, hamiltonian, couplings, gamma, coeff, node_count):
    device = jnp.repeat(jnp.arange(SHARDS, dtype=jnp.int32), NODE_DEV)
    slot = jnp.tile(jnp.arange(NODE_DEV, dtype=jnp.int32), SHARDS)
    live, first, second, found = hierarchy(node_count, device, slot)
    positions = jnp.stack([jnp.where(v, o * NODE_DEV + w, 0).astype(jnp.int32) for o, w, v in found], axis=1)
    valid = jnp.stack([v.astype(jnp.float32) for o, w, v in found], axis=1)
    levels = jnp.stack([first.astype(jnp.float32), second.astype(jnp.float32)], axis=1)
    alive = live.astype(jnp.float32)
    left_mat = jnp.concatenate([hamiltonian, couplings[0], couplings[1]], axis=1)
    right_mat = jnp.concatenate([hamiltonian, couplings[0], couplings[1]], axis=0)
    high = lax.Precision.HIGHEST

    def slope(state):

        def one(block):
            own, pos, val, lev, keep = block
            linked = [jnp.take(state, pos[:, j], axis=0) * val[:, j][:, None, None, None] for j in range(4)]
            lev_pair = (lev[:, 0], lev[:, 1])
            lefts = mixes(linked, lev_pair, coeff, 1.0)
            rights = mixes(linked, lev_pair, coeff, -1.0)
            left = jnp.einsum('ij,scjk->scik', left_mat, jnp.concatenate([own] + lefts, axis=2), precision=high)
            right = jnp.einsum('scij,jk->scik', jnp.concatenate([own] + rights, axis=3), right_mat, precision=high)
            comm = left - right
            damping = (lev[:, 0] * gamma[0] + lev[:, 1] * gamma[1])[:, None, None]
            out_re = comm[:, 1] - damping * own[:, 0]
            out_im = -comm[:, 0] - damping * own[:, 1]
            return jnp.stack([out_re, out_im], axis=1) * keep[:, None, None, None]
        blocks = (state.reshape(SHARDS, NODE_DEV, 2, D, D), positions.reshape(SHARDS, NODE_DEV, 4), valid.reshape(SHARDS, NODE_DEV, 4), levels.reshape(SHARDS, NODE_DEV, 2), alive.reshape(SHARDS, NODE_DEV))
        return lax.map(one, blocks).reshape(SLOTS, 2, D, D)
    first_slope = slope(densities)
    middle = densities + 0.5 * step_size * first_slope
    second_slope = slope(middle)
    return densities + step_size * second_slope
```

```python
import functools

import jax
import jax.numpy as jnp
from jax import lax
from jax.experimental import pallas as pl
from jax.experimental.pallas import tpu as pltpu
from jax.sharding import PartitionSpec as P

DEPTH2 = 2
REACH = 2 * DEPTH2
MESH = pl.DeviceIdType.MESH
step_size = 0.2
second = step_size * 0.5 * step_size


def split(value):
    high = value.astype(jnp.bfloat16)
    low = (value - high.astype(jnp.float32)).astype(jnp.bfloat16)
    return high, low


def product(high, low, rhs_high, rhs_low):
    rows = high.shape[0]
    both = jnp.concatenate([high, low], axis=0)
    wide = jnp.dot(both, rhs_high, preferred_element_type=jnp.float32)
    rest = jnp.dot(high, rhs_low, preferred_element_type=jnp.float32)
    return wide[:rows] + (wide[rows:] + rest)


def number(flag):
    return jnp.where(flag, jnp.float32(1), jnp.float32(0))


def kernel(
    shards,
    ring,
    counts,
    gamma,
    coeff,
    x_hbm,
    h_hbm,
    q_hbm,
    out_ref,
    x_ref,
    h_ref,
    q_ref,
    near_out,
    far_out,
    near_in,
    far_in,
    nodes,
    raised,
    right_high,
    right_low,
    mixed_high,
    mixed_low,
    turned,
    drive,
    decay,
    coupled,
    left_high,
    left_low,
    stack_high,
    stack_low,
    sums,
    own,
    from_left,
    from_right,
    hop_send,
    hop_recv,
    line_send,
    line_recv,
    load_sem,
):
    slots, _, rows, order = x_hbm.shape
    here = lax.axis_index("hier")
    me = lax.axis_index("col")
    has_lower = here > 0
    has_upper = here < shards - 1
    has_left = me > 0
    has_right = me < ring - 1
    f32 = jnp.float32

    loads = [
        pltpu.make_async_copy(source, place, load_sem.at[i])
        for i, (source, place) in enumerate(((x_hbm, x_ref), (h_hbm, h_ref), (q_hbm, q_ref)))
    ]
    for load in loads:
        load.start()

    barrier = pltpu.get_barrier_semaphore()
    neighbours = (
        (has_left, (here, me - 1)),
        (has_right, (here, me + 1)),
        (has_lower, (here - 1, me)),
        (has_upper, (here + 1, me)),
    )
    greeted = jnp.int32(0)
    for exists, device in neighbours:

        @pl.when(exists)
        def _():
            pl.semaphore_signal(barrier, inc=1, device_id=device, device_id_type=MESH)

        greeted = greeted + exists.astype(jnp.int32)
    pl.semaphore_wait(barrier, greeted)

    def hop_copy(stage, way):
        if stage == 0:
            source = near_out if way == 0 else x_hbm.at[pl.ds(0, DEPTH2)]
            place = near_in.at[way]
        else:
            source, place = far_out.at[way], far_in.at[way]
        return pltpu.make_async_remote_copy(
            src_ref=source,
            dst_ref=place,
            send_sem=hop_send.at[stage, way],
            recv_sem=hop_recv.at[stage, way],
            device_id=(here + 1, me) if way == 0 else (here - 1, me),
            device_id_type=MESH,
        )

    def hop_exists(way):
        return has_upper if way == 0 else has_lower

    def hop_comes(way):
        return has_lower if way == 0 else has_upper

    @pl.when(has_lower)
    def _():
        hop_copy(0, 1).start()

    for way in range(2):

        @pl.when(jnp.logical_not(hop_comes(way)))
        def _():
            near_in[way] = jnp.zeros(near_in.shape[1:], f32)
            far_in[way] = jnp.zeros(far_in.shape[1:], f32)

    offset = jnp.int32(0)
    total = jnp.int32(0)
    count = jnp.int32(0)
    for i in range(shards):
        held = counts[i]
        total = total + held
        offset = offset + jnp.where(here > i, held, 0)
        count = count + jnp.where(here == i, held, 0)
    live_total = total // DEPTH2 * DEPTH2
    tops = live_total // DEPTH2
    is_count = {c: number(count == c) for c in range(slots // 2, slots + 1)}

    def levels(k):
        node = offset + k
        level = (node + REACH) // DEPTH2 - REACH // DEPTH2
        return level, node - level * DEPTH2, number((node >= 0) & (node < live_total))

    def root(value):
        return jnp.sqrt(jnp.full((1, order), value, f32))

    zeroth, first, inside, damping = {}, {}, {}, {}
    for k in range(-REACH, slots + REACH):
        zeroth[k], first[k], inside[k] = levels(k)
        damping[k] = zeroth[k].astype(f32) * gamma[0] + first[k].astype(f32) * gamma[1]
    weights = {}
    for k in range(-DEPTH2, slots + DEPTH2):
        base = jnp.maximum(zeroth[k], 0).astype(f32)
        above = first[k].astype(f32)
        ok = number(first[k] + 1 < DEPTH2)
        weights[k, 0] = (
            root(base + 1.0) * (inside[k] * inside[k + DEPTH2]),
            root(base) * (inside[k] * inside[k - DEPTH2]),
        )
        weights[k, 1] = (
            root(above + 1.0) * (inside[k] * inside[k + 1] * ok),
            root(above) * (inside[k] * inside[k - 1]),
        )

    def mixes(array, shift, k, mode):
        stride = DEPTH2 if mode == 0 else 1
        rise, fall = weights[k, mode]
        up, down = k + stride + shift, k - stride + shift
        up_re, up_im = array[up, 0], array[up, 1]
        down_re, down_im = array[down, 0], array[down, 1]
        real, imag = fall * coeff[mode, 0], fall * coeff[mode, 1]
        base_re = rise * up_re + real * down_re
        base_im = rise * up_im + real * down_im
        turn_re, turn_im = imag * down_im, imag * down_re
        plain = (base_re - turn_re, base_im + turn_im)
        conjugate = (base_re + turn_re, base_im - turn_im)
        return plain, conjugate

    def put_mixed(k, a, value):
        for p in range(2):
            high, low = split(value[p])
            at = pl.ds(p * rows, rows), pl.ds(a * order, order)
            mixed_high[(k + DEPTH2,) + at] = high
            mixed_low[(k + DEPTH2,) + at] = low

    def right_product(k, size):
        at = k + DEPTH2
        value = product(
            mixed_high[at : at + size].reshape(size * 2 * rows, 3 * order),
            mixed_low[at : at + size].reshape(size * 2 * rows, 3 * order),
            right_high[...],
            right_low[...],
        )
        return value.reshape(size, 2, rows, order)

    loads[0].wait()
    for j in range(DEPTH2):
        for p in range(2):
            value = None
            for c in is_count:
                term = is_count[c] * x_ref[c - 1 - j, p]
                value = term if value is None else value + term
            near_out[j, p] = value

    @pl.when(has_upper)
    def _():
        hop_copy(0, 0).start()

    for load in loads[1:]:
        load.wait()

    mine = pl.ds(pl.multiple_of(me * rows, rows), rows)
    for a in range(3):
        high, low = split(h_ref[...] if a == 0 else q_ref[a - 1])
        right_high[a * order : (a + 1) * order] = high
        right_low[a * order : (a + 1) * order] = low
    factors = [h_ref[mine, :], q_ref[0, mine, :], q_ref[1, mine, :]]
    high, low = split(jnp.concatenate(factors, axis=0))
    twice = []
    for a in range(3):
        at = slice(a * order, (a + 1) * order)
        value = product(high, low, right_high[at], right_low[at])
        twice.append([value[b * rows : (b + 1) * rows] for b in range(3)])
    blocks = factors + [
        -second * twice[0][0],
        -second * (twice[0][1] + twice[1][0]),
        -second * (twice[0][2] + twice[2][0]),
        -second * (twice[1][2] + twice[2][1]),
        -second * twice[1][1],
        -second * twice[2][2],
    ]
    high, low = split(jnp.concatenate(blocks, axis=0).T)
    left_high[...] = high
    left_low[...] = low

    high, low = split(x_ref[...].reshape(slots * 2 * rows, order))
    for mode in range(2):
        at = slice((mode + 1) * order, (mode + 2) * order)
        value = product(high, low, right_high[at], right_low[at])
        coupled[mode] = value.reshape(slots, 2, rows, order)

    @pl.when(has_lower)
    def _():
        hop_copy(0, 0).wait_recv()

    for j in range(DEPTH2):
        for p in range(2):
            nodes[REACH - 1 - j, p] = near_in[0, j, p] * inside[-1 - j]
            nodes[REACH + j, p] = x_ref[j, p] * inside[j]
    for j in range(DEPTH2):
        for p in range(2):
            value = None
            for c in is_count:
                term = is_count[c] * nodes[REACH + c - 1 - DEPTH2 - j, p]
                value = term if value is None else value + term
            far_out[0, j, p] = value

    @pl.when(has_upper)
    def _():
        hop_copy(1, 0).start()
        hop_copy(0, 1).wait_recv()

    def upper_near(k, p):
        value = None
        for c in is_count:
            if 0 <= k - c < DEPTH2:
                term = is_count[c] * near_in[1, k - c, p]
                value = term if value is None else value + term
        return value

    def upper_far(k, p):
        value = None
        for c in is_count:
            if DEPTH2 <= k - c < REACH:
                term = is_count[c] * far_in[1, k - c - DEPTH2, p]
                value = term if value is None else value + term
        return value

    for k in range(DEPTH2, slots):
        for p in range(2):
            value = x_ref[k, p] * number(k < count) + upper_near(k, p)
            nodes[REACH + k, p] = value * inside[k]
            far_out[1, k - DEPTH2, p] = value

    @pl.when(has_lower)
    def _():
        hop_copy(1, 1).start()
        hop_copy(1, 0).wait_recv()

    @pl.when(has_upper)
    def _():
        hop_copy(1, 1).wait_recv()

    for j in range(DEPTH2):
        for p in range(2):
            nodes[REACH - 1 - DEPTH2 - j, p] = far_in[0, j, p] * inside[-1 - DEPTH2 - j]
    for k in range(slots, slots + REACH):
        for p in range(2):
            near, far = upper_near(k, p), upper_far(k, p)
            value = far if near is None else near if far is None else near + far
            nodes[REACH + k, p] = value * inside[k]

    wide = range(-DEPTH2, slots + DEPTH2)

    def put_stack(s, a, value):
        for p in range(2):
            high, low = split(value[p])
            at = pl.ds(a * rows, rows), pl.ds(p * order, order)
            stack_high[(s,) + at] = high
            stack_low[(s,) + at] = low

    for k in wide:
        plain, conjugate = mixes(nodes, REACH, k, 0)
        for p in range(2):
            raised[k + DEPTH2, p] = plain[p]
        put_mixed(k, 0, (nodes[k + REACH, 0], nodes[k + REACH, 1]))
        put_mixed(k, 1, conjugate)
        plain, conjugate = mixes(nodes, REACH, k, 1)
        put_mixed(k, 2, conjugate)
        if 0 <= k < slots:
            put_stack(k, 5, plain)
    turned[...] = right_product(-DEPTH2, slots + 2 * DEPTH2)

    for k in wide:
        at = k + DEPTH2
        beta = second * damping[k] - step_size
        x_re, x_im = nodes[k + REACH, 0], nodes[k + REACH, 1]
        drive[at, 0] = (2 * second) * turned[at, 0] - beta * x_im
        drive[at, 1] = (2 * second) * turned[at, 1] + beta * x_re
        decay[at, 0] = (second * damping[k]) * x_im - second * turned[at, 0]
        decay[at, 1] = -(second * damping[k]) * x_re - second * turned[at, 1]

    def line_copy(way, q, s):
        place = from_left if way == 0 else from_right
        return pltpu.make_async_remote_copy(
            src_ref=sums.at[s, pl.ds(q * rows, rows), :],
            dst_ref=place.at[q, s],
            send_sem=line_send.at[way, q, s],
            recv_sem=line_recv.at[way, q, s],
            device_id=(here, me + 1) if way == 0 else (here, me - 1),
            device_id_type=MESH,
        )

    for s in range(slots):
        at = s + DEPTH2
        tilt = second * damping[s]
        x_re, x_im = nodes[s + REACH, 0], nodes[s + REACH, 1]
        put_stack(s, 0, (drive[at, 0] - tilt * x_im, drive[at, 1] + tilt * x_re))
        top = zeroth[s].astype(f32)
        edge = (
            number(zeroth[s] + 1 < tops) * (top + 1.0) - top,
            number(first[s] + 1 < DEPTH2) * (first[s].astype(f32) + 1.0) - first[s].astype(f32),
        )
        for mode in range(2):
            plain, _ = mixes(drive, DEPTH2, s, mode)
            if mode == 0:
                linked = raised[at, 0], raised[at, 1]
            else:
                linked, _ = mixes(nodes, REACH, s, 1)
            turn = 2 * second * coeff[mode, 1] * edge[mode]
            put_stack(
                s,
                mode + 1,
                (
                    plain[0] - tilt * linked[1] - turn * coupled[mode, s, 1],
                    plain[1] + tilt * linked[0] + turn * coupled[mode, s, 0],
                ),
            )
        put_stack(s, 3, (x_re, x_im))
        put_stack(s, 4, (raised[at, 0], raised[at, 1]))
        plain, _ = mixes(raised, DEPTH2, s, 1)
        put_stack(s, 6, plain)
        plain, _ = mixes(raised, DEPTH2, s, 0)
        put_stack(s, 7, plain)
        real, imag = coeff[1, 0], coeff[1, 1]
        put_stack(s, 8, (real * x_re - imag * x_im, real * x_im + imag * x_re))
        high = stack_high[s]
        sums[s] = product(left_high[...], left_low[...], high, stack_low[s])

        @pl.when(jnp.logical_not(has_left))
        def _():
            line_copy(0, ring - 1, s).start()

        @pl.when(jnp.logical_not(has_right))
        def _():
            line_copy(1, 0, s).start()

    for i in range(1, ring - 1):
        for s in range(slots):

            @pl.when(jnp.logical_not(has_left))
            def _():
                line_copy(0, ring - 1 - i, s).start()

            @pl.when(jnp.logical_not(has_right))
            def _():
                line_copy(1, i, s).start()

    for s in range(slots):
        put_mixed(s, 0, (decay[s + DEPTH2, 0], decay[s + DEPTH2, 1]))
        for mode in range(2):
            _, conjugate = mixes(decay, DEPTH2, s, mode)
            put_mixed(s, mode + 1, conjugate)
    own[...] = right_product(0, slots)
    for s in range(slots):
        at = s + DEPTH2
        rate = damping[s]
        keep = 1.0 - step_size * rate + second * rate * rate
        beta = step_size - second * rate
        alive = inside[s] * number(s < count)
        own_re = own[s, 0] + keep * nodes[s + REACH, 0] - beta * turned[at, 1]
        own_im = own[s, 1] + keep * nodes[s + REACH, 1] + beta * turned[at, 0]
        out_ref[s, 0] = alive * (own_re + sums[s, mine, :order]) + (1.0 - alive) * x_ref[s, 0]
        out_ref[s, 1] = alive * (own_im + sums[s, mine, order:]) + (1.0 - alive) * x_ref[s, 1]

    def pass_on(way, q, s):
        place = from_left if way == 0 else from_right
        comes = has_left if way == 0 else has_right
        before = me < q if way == 0 else me > q
        line = pl.ds(q * rows, rows)

        @pl.when(comes & before)
        def _():
            line_copy(way, q, s).wait_recv()
            sums[s, line, :] = sums[s, line, :] + place[q, s]
            line_copy(way, q, s).start()

        @pl.when(comes & (me == q))
        def _():
            line_copy(way, q, s).wait_recv()
            alive = inside[s] * number(s < count)
            out_ref[s, 0] = out_ref[s, 0] + alive * place[q, s, :, :order]
            out_ref[s, 1] = out_ref[s, 1] + alive * place[q, s, :, order:]

    for i in range(ring - 1):
        for s in range(slots):
            pass_on(0, ring - 1 - i, s)
            pass_on(1, i, s)

    for stage in range(2):
        for way in range(2):

            @pl.when(hop_exists(way))
            def _():
                hop_copy(stage, way).wait_send()

    for i in range(ring - 1):
        for s in range(slots):

            @pl.when(me < ring - 1 - i)
            def _():
                line_copy(0, ring - 1 - i, s).wait_send()

            @pl.when(me > i)
            def _():
                line_copy(1, i, s).wait_send()


def solution(mesh):
    shards, ring = mesh.shape["hier"], mesh.shape["col"]

    def on_device(densities, hamiltonian, couplings, gamma, coeff, node_count):
        slots, _, rows, order = densities.shape
        f32, bf16 = jnp.float32, jnp.bfloat16
        vmem = pl.BlockSpec(memory_space=pltpu.VMEM)
        smem = pl.BlockSpec(memory_space=pltpu.SMEM)
        dma = pltpu.SemaphoreType.DMA
        wide = slots + 2 * DEPTH2
        block = (2, rows, order)
        return pl.pallas_call(
            functools.partial(kernel, shards, ring),
            out_shape=jax.ShapeDtypeStruct(densities.shape, f32),
            in_specs=[smem] * 3 + [pl.BlockSpec(memory_space=pltpu.HBM)] * 3,
            out_specs=vmem,
            scratch_shapes=[
                pltpu.VMEM((slots, *block), f32),
                pltpu.VMEM((order, order), f32),
                pltpu.VMEM((2, order, order), f32),
                pltpu.VMEM((DEPTH2, *block), f32),
                pltpu.VMEM((2, DEPTH2, *block), f32),
                pltpu.VMEM((2, DEPTH2, *block), f32),
                pltpu.VMEM((2, DEPTH2, *block), f32),
                pltpu.VMEM((slots + 2 * REACH, *block), f32),
                pltpu.VMEM((wide, *block), f32),
                pltpu.VMEM((3 * order, order), bf16),
                pltpu.VMEM((3 * order, order), bf16),
                pltpu.VMEM((wide, 2 * rows, 3 * order), bf16),
                pltpu.VMEM((wide, 2 * rows, 3 * order), bf16),
                pltpu.VMEM((wide, *block), f32),
                pltpu.VMEM((wide, *block), f32),
                pltpu.VMEM((wide, *block), f32),
                pltpu.VMEM((2, slots, *block), f32),
                pltpu.VMEM((order, 9 * rows), bf16),
                pltpu.VMEM((order, 9 * rows), bf16),
                pltpu.VMEM((slots, 9 * rows, 2 * order), bf16),
                pltpu.VMEM((slots, 9 * rows, 2 * order), bf16),
                pltpu.VMEM((slots, order, 2 * order), f32),
                pltpu.VMEM((slots, *block), f32),
                pltpu.VMEM((ring, slots, rows, 2 * order), f32),
                pltpu.VMEM((ring, slots, rows, 2 * order), f32),
                dma((2, 2)),
                dma((2, 2)),
                dma((2, ring, slots)),
                dma((2, ring, slots)),
                dma((3,)),
            ],
            compiler_params=pltpu.CompilerParams(
                collective_id=0, has_side_effects=True, vmem_limit_bytes=67_043_328
            ),
        )(node_count, gamma, coeff, densities, hamiltonian, couplings)

    return jax.shard_map(
        on_device,
        mesh=mesh,
        in_specs=(P("hier", None, "col", None), P(), P(), P(), P(), P()),
        out_specs=P("hier", None, "col", None),
        check_vma=False,
    )
```

```python
import functools

import jax
import jax.numpy as jnp
from jax import lax
from jax.experimental import pallas as pl
from jax.experimental.pallas import tpu as pltpu
from jax.sharding import PartitionSpec as P

DEPTH2 = 2
REACH = 2 * DEPTH2
WINDOW = 3
LAG = 2
MESH = pl.DeviceIdType.MESH
step_size = 0.2
second = step_size * 0.5 * step_size


def split(value):
    high = value.astype(jnp.bfloat16)
    low = (value - high.astype(jnp.float32)).astype(jnp.bfloat16)
    return high, low


def product(high, low, rhs_high, rhs_low):
    rows = high.shape[0]
    both = jnp.concatenate([high, low], axis=0)
    wide = jnp.dot(both, rhs_high, preferred_element_type=jnp.float32)
    rest = jnp.dot(high, rhs_low, preferred_element_type=jnp.float32)
    return wide[:rows] + (wide[rows:] + rest)


def number(flag):
    return jnp.where(flag, jnp.float32(1), jnp.float32(0))


def kernel(
    shards,
    ring,
    counts,
    gamma,
    coeff,
    x_hbm,
    h_hbm,
    q_hbm,
    out_ref,
    x_ref,
    h_ref,
    q_ref,
    near_out,
    far_out,
    near_in,
    far_in,
    nodes,
    raised,
    right_high,
    right_low,
    mixed_high,
    mixed_low,
    turned,
    drive,
    decay,
    coupled,
    left_high,
    left_low,
    stack_high,
    stack_low,
    sums,
    own,
    from_left,
    from_right,
    hop_send,
    hop_recv,
    line_send,
    line_recv,
    load_sem,
):
    slots, _, rows, order = x_hbm.shape
    here = lax.axis_index("hier")
    me = lax.axis_index("col")
    has_lower = here > 0
    has_upper = here < shards - 1
    has_left = me > 0
    has_right = me < ring - 1
    f32 = jnp.float32

    loads = [
        pltpu.make_async_copy(source, place, load_sem.at[i])
        for i, (source, place) in enumerate(((x_hbm, x_ref), (h_hbm, h_ref), (q_hbm, q_ref)))
    ]
    for load in loads:
        load.start()

    barrier = pltpu.get_barrier_semaphore()
    neighbours = (
        (has_left, (here, me - 1)),
        (has_right, (here, me + 1)),
        (has_lower, (here - 1, me)),
        (has_upper, (here + 1, me)),
    )
    greeted = jnp.int32(0)
    for exists, device in neighbours:

        @pl.when(exists)
        def _():
            pl.semaphore_signal(barrier, inc=1, device_id=device, device_id_type=MESH)

        greeted = greeted + exists.astype(jnp.int32)
    pl.semaphore_wait(barrier, greeted)

    def hop_copy(stage, way):
        if stage == 0:
            source = near_out if way == 0 else x_hbm.at[pl.ds(0, DEPTH2)]
            place = near_in.at[way]
        else:
            source, place = far_out.at[way], far_in.at[way]
        return pltpu.make_async_remote_copy(
            src_ref=source,
            dst_ref=place,
            send_sem=hop_send.at[stage, way],
            recv_sem=hop_recv.at[stage, way],
            device_id=(here + 1, me) if way == 0 else (here - 1, me),
            device_id_type=MESH,
        )

    def hop_exists(way):
        return has_upper if way == 0 else has_lower

    def hop_comes(way):
        return has_lower if way == 0 else has_upper

    @pl.when(has_lower)
    def _():
        hop_copy(0, 1).start()

    for way in range(2):

        @pl.when(jnp.logical_not(hop_comes(way)))
        def _():
            near_in[way] = jnp.zeros(near_in.shape[1:], f32)
            far_in[way] = jnp.zeros(far_in.shape[1:], f32)

    offset = jnp.int32(0)
    total = jnp.int32(0)
    count = jnp.int32(0)
    for i in range(shards):
        held = counts[i]
        total = total + held
        offset = offset + jnp.where(here > i, held, 0)
        count = count + jnp.where(here == i, held, 0)
    live_total = total // DEPTH2 * DEPTH2
    tops = live_total // DEPTH2
    is_count = {c: number(count == c) for c in range(slots // 2, slots + 1)}

    def levels(k):
        node = offset + k
        level = (node + REACH) // DEPTH2 - REACH // DEPTH2
        return level, node - level * DEPTH2, number((node >= 0) & (node < live_total))

    def root(value):
        return jnp.sqrt(jnp.full((1, order), value, f32))

    zeroth, first, inside, damping = {}, {}, {}, {}
    for k in range(-REACH, slots + REACH):
        zeroth[k], first[k], inside[k] = levels(k)
        damping[k] = zeroth[k].astype(f32) * gamma[0] + first[k].astype(f32) * gamma[1]
    weights = {}
    for k in range(-DEPTH2, slots + DEPTH2):
        base = jnp.maximum(zeroth[k], 0).astype(f32)
        above = first[k].astype(f32)
        ok = number(first[k] + 1 < DEPTH2)
        weights[k, 0] = (
            root(base + 1.0) * (inside[k] * inside[k + DEPTH2]),
            root(base) * (inside[k] * inside[k - DEPTH2]),
        )
        weights[k, 1] = (
            root(above + 1.0) * (inside[k] * inside[k + 1] * ok),
            root(above) * (inside[k] * inside[k - 1]),
        )

    def mixes(array, shift, k, mode):
        stride = DEPTH2 if mode == 0 else 1
        rise, fall = weights[k, mode]
        up, down = k + stride + shift, k - stride + shift
        up_re, up_im = array[up, 0], array[up, 1]
        down_re, down_im = array[down, 0], array[down, 1]
        real, imag = fall * coeff[mode, 0], fall * coeff[mode, 1]
        base_re = rise * up_re + real * down_re
        base_im = rise * up_im + real * down_im
        turn_re, turn_im = imag * down_im, imag * down_re
        plain = (base_re - turn_re, base_im + turn_im)
        conjugate = (base_re + turn_re, base_im - turn_im)
        return plain, conjugate

    def put_mixed(k, a, value):
        for p in range(2):
            high, low = split(value[p])
            at = pl.ds(p * rows, rows), pl.ds(a * order, order)
            mixed_high[(k + DEPTH2,) + at] = high
            mixed_low[(k + DEPTH2,) + at] = low

    def right_product(k, size):
        at = k + DEPTH2
        value = product(
            mixed_high[at : at + size].reshape(size * 2 * rows, 3 * order),
            mixed_low[at : at + size].reshape(size * 2 * rows, 3 * order),
            right_high[...],
            right_low[...],
        )
        return value.reshape(size, 2, rows, order)

    loads[0].wait()
    for j in range(DEPTH2):
        for p in range(2):
            value = None
            for c in is_count:
                term = is_count[c] * x_ref[c - 1 - j, p]
                value = term if value is None else value + term
            near_out[j, p] = value

    @pl.when(has_upper)
    def _():
        hop_copy(0, 0).start()

    for load in loads[1:]:
        load.wait()

    mine = pl.ds(pl.multiple_of(me * rows, rows), rows)
    for a in range(3):
        high, low = split(h_ref[...] if a == 0 else q_ref[a - 1])
        right_high[a * order : (a + 1) * order] = high
        right_low[a * order : (a + 1) * order] = low
    factors = [h_ref[mine, :], q_ref[0, mine, :], q_ref[1, mine, :]]
    high, low = split(jnp.concatenate(factors, axis=0))
    twice = []
    for a in range(3):
        at = slice(a * order, (a + 1) * order)
        value = product(high, low, right_high[at], right_low[at])
        twice.append([value[b * rows : (b + 1) * rows] for b in range(3)])
    parts = factors + [
        -second * twice[0][0],
        -second * (twice[0][1] + twice[1][0]),
        -second * (twice[0][2] + twice[2][0]),
        -second * (twice[1][2] + twice[2][1]),
        -second * twice[1][1],
        -second * twice[2][2],
    ]
    high, low = split(jnp.concatenate(parts, axis=0).T)
    left_high[...] = high
    left_low[...] = low

    high, low = split(x_ref[...].reshape(slots * 2 * rows, order))
    for mode in range(2):
        at = slice((mode + 1) * order, (mode + 2) * order)
        value = product(high, low, right_high[at], right_low[at])
        coupled[mode] = value.reshape(slots, 2, rows, order)

    @pl.when(has_lower)
    def _():
        hop_copy(0, 0).wait_recv()

    for j in range(DEPTH2):
        for p in range(2):
            nodes[REACH - 1 - j, p] = near_in[0, j, p] * inside[-1 - j]
            nodes[REACH + j, p] = x_ref[j, p] * inside[j]
    for j in range(DEPTH2):
        for p in range(2):
            value = None
            for c in is_count:
                term = is_count[c] * nodes[REACH + c - 1 - DEPTH2 - j, p]
                value = term if value is None else value + term
            far_out[0, j, p] = value

    @pl.when(has_upper)
    def _():
        hop_copy(1, 0).start()
        hop_copy(0, 1).wait_recv()

    def upper_near(k, p):
        value = None
        for c in is_count:
            if 0 <= k - c < DEPTH2:
                term = is_count[c] * near_in[1, k - c, p]
                value = term if value is None else value + term
        return value

    def upper_far(k, p):
        value = None
        for c in is_count:
            if DEPTH2 <= k - c < REACH:
                term = is_count[c] * far_in[1, k - c - DEPTH2, p]
                value = term if value is None else value + term
        return value

    for k in range(DEPTH2, slots):
        for p in range(2):
            value = x_ref[k, p] * number(k < count) + upper_near(k, p)
            nodes[REACH + k, p] = value * inside[k]
            far_out[1, k - DEPTH2, p] = value

    @pl.when(has_lower)
    def _():
        hop_copy(1, 1).start()
        hop_copy(1, 0).wait_recv()

    @pl.when(has_upper)
    def _():
        hop_copy(1, 1).wait_recv()

    for j in range(DEPTH2):
        for p in range(2):
            nodes[REACH - 1 - DEPTH2 - j, p] = far_in[0, j, p] * inside[-1 - DEPTH2 - j]
    for k in range(slots, slots + REACH):
        for p in range(2):
            near, far = upper_near(k, p), upper_far(k, p)
            value = far if near is None else near if far is None else near + far
            nodes[REACH + k, p] = value * inside[k]

    wide = range(-DEPTH2, slots + DEPTH2)

    def put_stack(s, a, value):
        for p in range(2):
            high, low = split(value[p])
            at = pl.ds(a * rows, rows), pl.ds(p * order, order)
            stack_high[(s,) + at] = high
            stack_low[(s,) + at] = low

    for k in wide:
        plain, conjugate = mixes(nodes, REACH, k, 0)
        for p in range(2):
            raised[k + DEPTH2, p] = plain[p]
        put_mixed(k, 0, (nodes[k + REACH, 0], nodes[k + REACH, 1]))
        put_mixed(k, 1, conjugate)
        plain, conjugate = mixes(nodes, REACH, k, 1)
        put_mixed(k, 2, conjugate)
        if 0 <= k < slots:
            put_stack(k, 5, plain)
    turned[...] = right_product(-DEPTH2, slots + 2 * DEPTH2)

    for k in wide:
        at = k + DEPTH2
        beta = second * damping[k] - step_size
        x_re, x_im = nodes[k + REACH, 0], nodes[k + REACH, 1]
        drive[at, 0] = (2 * second) * turned[at, 0] - beta * x_im
        drive[at, 1] = (2 * second) * turned[at, 1] + beta * x_re
        decay[at, 0] = (second * damping[k]) * x_im - second * turned[at, 0]
        decay[at, 1] = -(second * damping[k]) * x_re - second * turned[at, 1]

    def panel(q):
        return pl.ds(pl.multiple_of(q * rows, rows), rows)

    def line_copy(way, q, s):
        place = from_left if way == 0 else from_right
        return pltpu.make_async_remote_copy(
            src_ref=sums.at[s, panel(q), :],
            dst_ref=place.at[q, s],
            send_sem=line_send.at[way, q, s],
            recv_sem=line_recv.at[way, q, s],
            device_id=(here, me + 1) if way == 0 else (here, me - 1),
            device_id_type=MESH,
        )

    blocks = (ring - 1) * slots

    def end_copy(way, j):
        q = j // slots
        return line_copy(way, ring - 1 - q if way == 0 else q, lax.rem(j, slots))

    def feed_one(way, j):
        @pl.when((j >= WINDOW) & (j < blocks + WINDOW))
        def _():
            end_copy(way, j - WINDOW).wait_send()

        @pl.when(j < blocks)
        def _():
            end_copy(way, j).start()

    def feed(j):
        for way, inner in ((0, has_left), (1, has_right)):

            @pl.when(jnp.logical_not(inner))
            def _():
                feed_one(way, jnp.int32(j))

    for s in range(slots):
        at = s + DEPTH2
        tilt = second * damping[s]
        x_re, x_im = nodes[s + REACH, 0], nodes[s + REACH, 1]
        put_stack(s, 0, (drive[at, 0] - tilt * x_im, drive[at, 1] + tilt * x_re))
        top = zeroth[s].astype(f32)
        edge = (
            number(zeroth[s] + 1 < tops) * (top + 1.0) - top,
            number(first[s] + 1 < DEPTH2) * (first[s].astype(f32) + 1.0) - first[s].astype(f32),
        )
        for mode in range(2):
            plain, _ = mixes(drive, DEPTH2, s, mode)
            if mode == 0:
                linked = raised[at, 0], raised[at, 1]
            else:
                linked, _ = mixes(nodes, REACH, s, 1)
            turn = 2 * second * coeff[mode, 1] * edge[mode]
            put_stack(
                s,
                mode + 1,
                (
                    plain[0] - tilt * linked[1] - turn * coupled[mode, s, 1],
                    plain[1] + tilt * linked[0] + turn * coupled[mode, s, 0],
                ),
            )
        put_stack(s, 3, (x_re, x_im))
        put_stack(s, 4, (raised[at, 0], raised[at, 1]))
        plain, _ = mixes(raised, DEPTH2, s, 1)
        put_stack(s, 6, plain)
        plain, _ = mixes(raised, DEPTH2, s, 0)
        put_stack(s, 7, plain)
        real, imag = coeff[1, 0], coeff[1, 1]
        put_stack(s, 8, (real * x_re - imag * x_im, real * x_im + imag * x_re))
        high = stack_high[s]
        sums[s] = product(left_high[...], left_low[...], high, stack_low[s])

        feed(s)

    for s in range(slots):
        put_mixed(s, 0, (decay[s + DEPTH2, 0], decay[s + DEPTH2, 1]))
        for mode in range(2):
            _, conjugate = mixes(decay, DEPTH2, s, mode)
            put_mixed(s, mode + 1, conjugate)
    own[...] = right_product(0, slots)
    for s in range(slots):
        at = s + DEPTH2
        rate = damping[s]
        keep = 1.0 - step_size * rate + second * rate * rate
        beta = step_size - second * rate
        alive = inside[s] * number(s < count)
        own_re = own[s, 0] + keep * nodes[s + REACH, 0] - beta * turned[at, 1]
        own_im = own[s, 1] + keep * nodes[s + REACH, 1] + beta * turned[at, 0]
        out_ref[s, 0] = alive * (own_re + sums[s, mine, :order]) + (1.0 - alive) * x_ref[s, 0]
        out_ref[s, 1] = alive * (own_im + sums[s, mine, order:]) + (1.0 - alive) * x_ref[s, 1]

    def pass_on(way, t):
        place = from_left if way == 0 else from_right
        passed = me if way == 0 else ring - 1 - me
        j = t - LAG * passed
        inner = (passed > 0) & (j >= 0)
        s = lax.rem(jnp.maximum(j, 0), slots)
        step = jnp.maximum(j, 0) // slots
        q = ring - 1 - step if way == 0 else step

        @pl.when(inner & (step < ring - 1 - passed))
        def _():
            line = panel(q)
            line_copy(way, q, s).wait_recv()
            sums[s, line, :] = sums[s, line, :] + place[q, s]
            line_copy(way, q, s).start()

        @pl.when(inner & (step == ring - 1 - passed))
        def _():
            line_copy(way, q, s).wait_recv()
            alive = number((offset + s < live_total) & (s < count))
            out_ref[s, 0] = out_ref[s, 0] + alive * place[q, s, :, :order]
            out_ref[s, 1] = out_ref[s, 1] + alive * place[q, s, :, order:]

    def advance(t, carry):
        for way, passed in ((0, me), (1, ring - 1 - me)):

            @pl.when((passed == 0) & (t >= slots))
            def _():
                feed_one(way, t)

        for way in range(2):
            pass_on(way, t)
        return carry

    lax.fori_loop(0, blocks + max(WINDOW, LAG * (ring - 1)), advance, 0)

    for stage in range(2):
        for way in range(2):

            @pl.when(hop_exists(way))
            def _():
                hop_copy(stage, way).wait_send()

    for i in range(ring - 1):
        for s in range(slots):

            @pl.when(has_left & (me < ring - 1 - i))
            def _():
                line_copy(0, ring - 1 - i, s).wait_send()

            @pl.when(has_right & (me > i))
            def _():
                line_copy(1, i, s).wait_send()


def solution(mesh):
    shards, ring = mesh.shape["hier"], mesh.shape["col"]

    def on_device(densities, hamiltonian, couplings, gamma, coeff, node_count):
        slots, _, rows, order = densities.shape
        f32, bf16 = jnp.float32, jnp.bfloat16
        vmem = pl.BlockSpec(memory_space=pltpu.VMEM)
        smem = pl.BlockSpec(memory_space=pltpu.SMEM)
        dma = pltpu.SemaphoreType.DMA
        wide = slots + 2 * DEPTH2
        block = (2, rows, order)
        return pl.pallas_call(
            functools.partial(kernel, shards, ring),
            out_shape=jax.ShapeDtypeStruct(densities.shape, f32),
            in_specs=[smem] * 3 + [pl.BlockSpec(memory_space=pltpu.HBM)] * 3,
            out_specs=vmem,
            scratch_shapes=[
                pltpu.VMEM((slots, *block), f32),
                pltpu.VMEM((order, order), f32),
                pltpu.VMEM((2, order, order), f32),
                pltpu.VMEM((DEPTH2, *block), f32),
                pltpu.VMEM((2, DEPTH2, *block), f32),
                pltpu.VMEM((2, DEPTH2, *block), f32),
                pltpu.VMEM((2, DEPTH2, *block), f32),
                pltpu.VMEM((slots + 2 * REACH, *block), f32),
                pltpu.VMEM((wide, *block), f32),
                pltpu.VMEM((3 * order, order), bf16),
                pltpu.VMEM((3 * order, order), bf16),
                pltpu.VMEM((wide, 2 * rows, 3 * order), bf16),
                pltpu.VMEM((wide, 2 * rows, 3 * order), bf16),
                pltpu.VMEM((wide, *block), f32),
                pltpu.VMEM((wide, *block), f32),
                pltpu.VMEM((wide, *block), f32),
                pltpu.VMEM((2, slots, *block), f32),
                pltpu.VMEM((order, 9 * rows), bf16),
                pltpu.VMEM((order, 9 * rows), bf16),
                pltpu.VMEM((slots, 9 * rows, 2 * order), bf16),
                pltpu.VMEM((slots, 9 * rows, 2 * order), bf16),
                pltpu.VMEM((slots, order, 2 * order), f32),
                pltpu.VMEM((slots, *block), f32),
                pltpu.VMEM((ring, slots, rows, 2 * order), f32),
                pltpu.VMEM((ring, slots, rows, 2 * order), f32),
                dma((2, 2)),
                dma((2, 2)),
                dma((2, ring, slots)),
                dma((2, ring, slots)),
                dma((3,)),
            ],
            compiler_params=pltpu.CompilerParams(
                collective_id=0, has_side_effects=True, vmem_limit_bytes=67_043_328
            ),
        )(node_count, gamma, coeff, densities, hamiltonian, couplings)

    return jax.shard_map(
        on_device,
        mesh=mesh,
        in_specs=(P("hier", None, "col", None), P(), P(), P(), P(), P()),
        out_specs=P("hier", None, "col", None),
        check_vma=False,
    )
```

```python
import functools

import jax
import jax.numpy as jnp
from jax import lax
from jax.experimental import pallas as pl
from jax.experimental.pallas import tpu as pltpu
from jax.sharding import PartitionSpec as P

DEPTH2 = 2
REACH = 2 * DEPTH2
WINDOW = 3
LAG = 2
NEAR_AT = 3
FAR_AT = 6
MESH = pl.DeviceIdType.MESH
step_size = 0.2
second = step_size * 0.5 * step_size


def split(value):
    high = value.astype(jnp.bfloat16)
    low = (value - high.astype(jnp.float32)).astype(jnp.bfloat16)
    return high, low


def product(high, low, rhs_high, rhs_low):
    rows = high.shape[0]
    both = jnp.concatenate([high, low], axis=0)
    wide = jnp.dot(both, rhs_high, preferred_element_type=jnp.float32)
    rest = jnp.dot(high, rhs_low, preferred_element_type=jnp.float32)
    return wide[:rows] + (wide[rows:] + rest)


def number(flag):
    return jnp.where(flag, jnp.float32(1), jnp.float32(0))


def kernel(
    shards,
    ring,
    counts,
    gamma,
    coeff,
    x_hbm,
    h_hbm,
    q_hbm,
    out_ref,
    x_ref,
    h_ref,
    q_ref,
    near_out,
    far_out,
    near_in,
    far_in,
    nodes,
    raised,
    right_high,
    right_low,
    mixed_high,
    mixed_low,
    turned,
    drive,
    decay,
    coupled,
    left_high,
    left_low,
    raw_in,
    stack_high,
    stack_low,
    sums,
    own,
    from_left,
    from_right,
    raw_send,
    raw_recv,
    hop_send,
    hop_recv,
    line_send,
    line_recv,
    load_sem,
):
    slots, _, rows, order = x_hbm.shape
    here = lax.axis_index("hier")
    me = lax.axis_index("col")
    has_lower = here > 0
    has_upper = here < shards - 1
    has_left = me > 0
    has_right = me < ring - 1
    f32 = jnp.float32

    loads = [
        pltpu.make_async_copy(source, place, load_sem.at[i])
        for i, (source, place) in enumerate(((x_hbm, x_ref), (h_hbm, h_ref), (q_hbm, q_ref)))
    ]
    for load in loads:
        load.start()

    barrier = pltpu.get_barrier_semaphore()
    neighbours = (
        (has_left, (here, me - 1)),
        (has_right, (here, me + 1)),
        (has_lower, (here - 1, me)),
        (has_upper, (here + 1, me)),
    )
    greeted = jnp.int32(0)
    for exists, device in neighbours:

        @pl.when(exists)
        def _():
            pl.semaphore_signal(barrier, inc=1, device_id=device, device_id_type=MESH)

        greeted = greeted + exists.astype(jnp.int32)
    pl.semaphore_wait(barrier, greeted)

    edge = (me == 1) | (me == ring - 2)
    end = jnp.where(me == 1, 0, ring - 1)

    def raw_copy(s):
        return pltpu.make_async_remote_copy(
            src_ref=x_hbm.at[s],
            dst_ref=raw_in.at[s],
            send_sem=raw_send.at[s],
            recv_sem=raw_recv.at[s],
            device_id=(here, jnp.where(me == 0, 1, ring - 2)),
            device_id_type=MESH,
        )

    def hop_copy(turn, stage, way):
        if stage == 0:
            first = (x_hbm if turn == 0 else raw_in).at[pl.ds(0, DEPTH2)]
            source = near_out.at[turn] if way == 0 else first
            place = near_in.at[turn, way]
        else:
            source, place = far_out.at[turn, way], far_in.at[turn, way]
        return pltpu.make_async_remote_copy(
            src_ref=source,
            dst_ref=place,
            send_sem=hop_send.at[turn, stage, way],
            recv_sem=hop_recv.at[turn, stage, way],
            device_id=(here + 1, me) if way == 0 else (here - 1, me),
            device_id_type=MESH,
        )

    def hop_exists(way):
        return has_upper if way == 0 else has_lower

    def hop_comes(way):
        return has_lower if way == 0 else has_upper

    @pl.when(has_lower)
    def _():
        hop_copy(0, 0, 1).start()

    @pl.when(jnp.logical_not(has_left & has_right))
    def _():
        for s in range(slots):
            raw_copy(s).start()

    for turn in range(2):
        for way in range(2):

            @pl.when(jnp.logical_not(hop_comes(way)))
            def _():
                near_in[turn, way] = jnp.zeros(near_in.shape[2:], f32)
                far_in[turn, way] = jnp.zeros(far_in.shape[2:], f32)

    offset = jnp.int32(0)
    total = jnp.int32(0)
    count = jnp.int32(0)
    for i in range(shards):
        held = counts[i]
        total = total + held
        offset = offset + jnp.where(here > i, held, 0)
        count = count + jnp.where(here == i, held, 0)
    live_total = total // DEPTH2 * DEPTH2
    tops = live_total // DEPTH2
    is_count = {c: number(count == c) for c in range(slots // 2, slots + 1)}

    def levels(k):
        node = offset + k
        level = (node + REACH) // DEPTH2 - REACH // DEPTH2
        return level, node - level * DEPTH2, number((node >= 0) & (node < live_total))

    def root(value):
        return jnp.sqrt(jnp.full((1, order), value, f32))

    zeroth, first, inside, damping = {}, {}, {}, {}
    for k in range(-REACH, slots + REACH):
        zeroth[k], first[k], inside[k] = levels(k)
        damping[k] = zeroth[k].astype(f32) * gamma[0] + first[k].astype(f32) * gamma[1]
    weights = {}
    for k in range(-DEPTH2, slots + DEPTH2):
        base = jnp.maximum(zeroth[k], 0).astype(f32)
        above = first[k].astype(f32)
        ok = number(first[k] + 1 < DEPTH2)
        weights[k, 0] = (
            root(base + 1.0) * (inside[k] * inside[k + DEPTH2]),
            root(base) * (inside[k] * inside[k - DEPTH2]),
        )
        weights[k, 1] = (
            root(above + 1.0) * (inside[k] * inside[k + 1] * ok),
            root(above) * (inside[k] * inside[k - 1]),
        )

    def mixes(array, shift, k, mode):
        stride = DEPTH2 if mode == 0 else 1
        rise, fall = weights[k, mode]
        up, down = k + stride + shift, k - stride + shift
        up_re, up_im = array[up, 0], array[up, 1]
        down_re, down_im = array[down, 0], array[down, 1]
        real, imag = fall * coeff[mode, 0], fall * coeff[mode, 1]
        base_re = rise * up_re + real * down_re
        base_im = rise * up_im + real * down_im
        turn_re, turn_im = imag * down_im, imag * down_re
        plain = (base_re - turn_re, base_im + turn_im)
        conjugate = (base_re + turn_re, base_im - turn_im)
        return plain, conjugate

    def put_mixed(k, a, value):
        for p in range(2):
            high, low = split(value[p])
            at = pl.ds(p * rows, rows), pl.ds(a * order, order)
            mixed_high[(k + DEPTH2,) + at] = high
            mixed_low[(k + DEPTH2,) + at] = low

    def right_product(k, size):
        at = k + DEPTH2
        value = product(
            mixed_high[at : at + size].reshape(size * 2 * rows, 3 * order),
            mixed_low[at : at + size].reshape(size * 2 * rows, 3 * order),
            right_high[...],
            right_low[...],
        )
        return value.reshape(size, 2, rows, order)

    def send_near(turn, state):
        for j in range(DEPTH2):
            for p in range(2):
                value = None
                for c in is_count:
                    term = is_count[c] * state[c - 1 - j, p]
                    value = term if value is None else value + term
                near_out[turn, j, p] = value

        @pl.when(has_upper)
        def _():
            hop_copy(turn, 0, 0).start()

    loads[0].wait()
    send_near(0, x_ref)

    for load in loads[1:]:
        load.wait()

    mine = pl.ds(pl.multiple_of(me * rows, rows), rows)
    for a in range(3):
        high, low = split(h_ref[...] if a == 0 else q_ref[a - 1])
        right_high[a * order : (a + 1) * order] = high
        right_low[a * order : (a + 1) * order] = low

    def left_factors(turn, lines):
        factors = [h_ref[lines, :], q_ref[0, lines, :], q_ref[1, lines, :]]
        high, low = split(jnp.concatenate(factors, axis=0))
        twice = []
        for a in range(3):
            at = slice(a * order, (a + 1) * order)
            value = product(high, low, right_high[at], right_low[at])
            twice.append([value[b * rows : (b + 1) * rows] for b in range(3)])
        parts = factors + [
            -second * twice[0][0],
            -second * (twice[0][1] + twice[1][0]),
            -second * (twice[0][2] + twice[2][0]),
            -second * (twice[1][2] + twice[2][1]),
            -second * twice[1][1],
            -second * twice[2][2],
        ]
        high, low = split(jnp.concatenate(parts, axis=0).T)
        left_high[turn] = high
        left_low[turn] = low

    left_factors(0, mine)

    @pl.when(edge)
    def _():
        left_factors(1, pl.ds(pl.multiple_of(end * rows, rows), rows))

    def couple(state):
        high, low = split(state[...].reshape(slots * 2 * rows, order))
        for mode in range(2):
            at = slice((mode + 1) * order, (mode + 2) * order)
            value = product(high, low, right_high[at], right_low[at])
            coupled[mode] = value.reshape(slots, 2, rows, order)

    couple(x_ref)

    def upper_near(turn, k, p):
        value = None
        for c in is_count:
            if 0 <= k - c < DEPTH2:
                term = is_count[c] * near_in[turn, 1, k - c, p]
                value = term if value is None else value + term
        return value

    def upper_far(turn, k, p):
        value = None
        for c in is_count:
            if DEPTH2 <= k - c < REACH:
                term = is_count[c] * far_in[turn, 1, k - c - DEPTH2, p]
                value = term if value is None else value + term
        return value

    def gather_near(turn, state):
        @pl.when(has_lower)
        def _():
            hop_copy(turn, 0, 0).wait_recv()

        for j in range(DEPTH2):
            for p in range(2):
                nodes[REACH - 1 - j, p] = near_in[turn, 0, j, p] * inside[-1 - j]
                nodes[REACH + j, p] = state[j, p] * inside[j]
        for j in range(DEPTH2):
            for p in range(2):
                value = None
                for c in is_count:
                    term = is_count[c] * nodes[REACH + c - 1 - DEPTH2 - j, p]
                    value = term if value is None else value + term
                far_out[turn, 0, j, p] = value

        @pl.when(has_upper)
        def _():
            hop_copy(turn, 1, 0).start()
            hop_copy(turn, 0, 1).wait_recv()

        for k in range(DEPTH2, slots):
            for p in range(2):
                value = state[k, p] * number(k < count) + upper_near(turn, k, p)
                nodes[REACH + k, p] = value * inside[k]
                far_out[turn, 1, k - DEPTH2, p] = value

        @pl.when(has_lower)
        def _():
            hop_copy(turn, 1, 1).start()

    def gather_far(turn):
        @pl.when(has_lower)
        def _():
            hop_copy(turn, 1, 0).wait_recv()

        @pl.when(has_upper)
        def _():
            hop_copy(turn, 1, 1).wait_recv()

        for j in range(DEPTH2):
            for p in range(2):
                at = REACH - 1 - DEPTH2 - j
                nodes[at, p] = far_in[turn, 0, j, p] * inside[-1 - DEPTH2 - j]
        for k in range(slots, slots + REACH):
            for p in range(2):
                near, far = upper_near(turn, k, p), upper_far(turn, k, p)
                value = far if near is None else near if far is None else near + far
                nodes[REACH + k, p] = value * inside[k]

    wide = range(-DEPTH2, slots + DEPTH2)

    def put_stack(s, a, value):
        for p in range(2):
            high, low = split(value[p])
            at = pl.ds(a * rows, rows), pl.ds(p * order, order)
            stack_high[(s,) + at] = high
            stack_low[(s,) + at] = low

    def mix_nodes():
        for k in wide:
            plain, conjugate = mixes(nodes, REACH, k, 0)
            for p in range(2):
                raised[k + DEPTH2, p] = plain[p]
            put_mixed(k, 0, (nodes[k + REACH, 0], nodes[k + REACH, 1]))
            put_mixed(k, 1, conjugate)
            plain, conjugate = mixes(nodes, REACH, k, 1)
            put_mixed(k, 2, conjugate)
            if 0 <= k < slots:
                put_stack(k, 5, plain)

    def turn_nodes(first, size):
        turned[first + DEPTH2 : first + DEPTH2 + size] = right_product(first, size)
        for k in range(first, first + size):
            at = k + DEPTH2
            beta = second * damping[k] - step_size
            x_re, x_im = nodes[k + REACH, 0], nodes[k + REACH, 1]
            drive[at, 0] = (2 * second) * turned[at, 0] - beta * x_im
            drive[at, 1] = (2 * second) * turned[at, 1] + beta * x_re

    gather_near(0, x_ref)
    gather_far(0)
    mix_nodes()
    turn_nodes(-DEPTH2, slots + 2 * DEPTH2)

    @pl.when(edge)
    def _():
        for s in range(slots):
            raw_copy(s).wait_recv()

        @pl.when(has_lower)
        def _():
            hop_copy(1, 0, 1).start()

        send_near(1, raw_in)

    def panel(q):
        return pl.ds(pl.multiple_of(q * rows, rows), rows)

    def line_copy(way, q, s):
        place = from_left if way == 0 else from_right
        return pltpu.make_async_remote_copy(
            src_ref=sums.at[s, panel(q), :],
            dst_ref=place.at[q, s],
            send_sem=line_send.at[way, q, s],
            recv_sem=line_recv.at[way, q, s],
            device_id=(here, me + 1) if way == 0 else (here, me - 1),
            device_id_type=MESH,
        )

    blocks = (ring - 2) * slots

    def end_copy(way, j):
        q = j // slots
        return line_copy(way, ring - 1 - q if way == 0 else q, lax.rem(j, slots))

    def feed_one(way, j):
        @pl.when((j >= WINDOW) & (j < blocks + WINDOW))
        def _():
            end_copy(way, j - WINDOW).wait_send()

        @pl.when(j < blocks)
        def _():
            end_copy(way, j).start()

    def feed(j):
        for way, inner in ((0, has_left), (1, has_right)):

            @pl.when(jnp.logical_not(inner))
            def _():
                feed_one(way, jnp.int32(j))

    def fill_stack(s):
        at = s + DEPTH2
        tilt = second * damping[s]
        x_re, x_im = nodes[s + REACH, 0], nodes[s + REACH, 1]
        put_stack(s, 0, (drive[at, 0] - tilt * x_im, drive[at, 1] + tilt * x_re))
        top = zeroth[s].astype(f32)
        lift = (
            number(zeroth[s] + 1 < tops) * (top + 1.0) - top,
            number(first[s] + 1 < DEPTH2) * (first[s].astype(f32) + 1.0) - first[s].astype(f32),
        )
        for mode in range(2):
            plain, _ = mixes(drive, DEPTH2, s, mode)
            if mode == 0:
                linked = raised[at, 0], raised[at, 1]
            else:
                linked, _ = mixes(nodes, REACH, s, 1)
            turn = 2 * second * coeff[mode, 1] * lift[mode]
            put_stack(
                s,
                mode + 1,
                (
                    plain[0] - tilt * linked[1] - turn * coupled[mode, s, 1],
                    plain[1] + tilt * linked[0] + turn * coupled[mode, s, 0],
                ),
            )
        put_stack(s, 3, (x_re, x_im))
        put_stack(s, 4, (raised[at, 0], raised[at, 1]))
        plain, _ = mixes(raised, DEPTH2, s, 1)
        put_stack(s, 6, plain)
        plain, _ = mixes(raised, DEPTH2, s, 0)
        put_stack(s, 7, plain)
        real, imag = coeff[1, 0], coeff[1, 1]
        put_stack(s, 8, (real * x_re - imag * x_im, real * x_im + imag * x_re))

    for s in range(slots):
        fill_stack(s)
        sums[s] = product(left_high[0], left_low[0], stack_high[s], stack_low[s])
        feed(s)

    for k in wide:
        at = k + DEPTH2
        x_re, x_im = nodes[k + REACH, 0], nodes[k + REACH, 1]
        decay[at, 0] = (second * damping[k]) * x_im - second * turned[at, 0]
        decay[at, 1] = -(second * damping[k]) * x_re - second * turned[at, 1]
    for s in range(slots):
        put_mixed(s, 0, (decay[s + DEPTH2, 0], decay[s + DEPTH2, 1]))
        for mode in range(2):
            _, conjugate = mixes(decay, DEPTH2, s, mode)
            put_mixed(s, mode + 1, conjugate)
    own[...] = right_product(0, slots)
    for s in range(slots):
        at = s + DEPTH2
        rate = damping[s]
        keep = 1.0 - step_size * rate + second * rate * rate
        beta = step_size - second * rate
        alive = inside[s] * number(s < count)
        own_re = own[s, 0] + keep * nodes[s + REACH, 0] - beta * turned[at, 1]
        own_im = own[s, 1] + keep * nodes[s + REACH, 1] + beta * turned[at, 0]
        out_ref[s, 0] = alive * (own_re + sums[s, mine, :order]) + (1.0 - alive) * x_ref[s, 0]
        out_ref[s, 1] = alive * (own_im + sums[s, mine, order:]) + (1.0 - alive) * x_ref[s, 1]

    def pass_on(way, t):
        place = from_left if way == 0 else from_right
        passed = me if way == 0 else ring - 1 - me
        j = t - LAG * passed
        inner = (passed > 0) & (j >= 0) & (j < blocks)
        s = lax.rem(jnp.maximum(j, 0), slots)
        step = jnp.maximum(j, 0) // slots
        q = ring - 1 - step if way == 0 else step

        @pl.when(inner & (step < ring - 1 - passed))
        def _():
            line = panel(q)
            line_copy(way, q, s).wait_recv()
            sums[s, line, :] = sums[s, line, :] + place[q, s]
            line_copy(way, q, s).start()

        @pl.when(inner & (step == ring - 1 - passed))
        def _():
            line_copy(way, q, s).wait_recv()
            alive = number((offset + s < live_total) & (s < count))
            out_ref[s, 0] = out_ref[s, 0] + alive * place[q, s, :, :order]
            out_ref[s, 1] = out_ref[s, 1] + alive * place[q, s, :, order:]

    def advance(t, carry):
        for way, passed in ((0, me), (1, ring - 1 - me)):

            @pl.when((passed == 0) & (t >= slots))
            def _():
                feed_one(way, t)

        for way in range(2):
            pass_on(way, t)
        return carry

    def act(s):
        fill_stack(s)
        value = product(left_high[1, mine, :], left_low[1, mine, :], stack_high[s], stack_low[s])
        alive = inside[s] * number(s < count)
        out_ref[s, 0] = out_ref[s, 0] + alive * value[:, :order]
        out_ref[s, 1] = out_ref[s, 1] + alive * value[:, order:]

    def extra_near():
        gather_near(1, raw_in)
        couple(raw_in)

    def extra_far():
        gather_far(1)
        mix_nodes()

    half = slots // 2 + DEPTH2
    extras = (
        (NEAR_AT, extra_near),
        (FAR_AT, extra_far),
        (FAR_AT + 1, functools.partial(turn_nodes, -DEPTH2, half)),
        (FAR_AT + 2, functools.partial(turn_nodes, half - DEPTH2, half)),
        (FAR_AT + 3, lambda: [act(s) for s in range(slots // 2)]),
        (FAR_AT + 4, lambda: [act(s) for s in range(slots // 2, slots)]),
    )
    begin = 0
    for at, extra in extras:
        lax.fori_loop(begin, at, advance, 0)
        begin = at

        @pl.when(edge)
        def _():
            extra()

    lax.fori_loop(begin, blocks + max(WINDOW, LAG * (ring - 1)), advance, 0)

    @pl.when(jnp.logical_not(has_left & has_right))
    def _():
        for s in range(slots):
            raw_copy(s).wait_send()

    for stage in range(2):
        for way in range(2):

            @pl.when(hop_exists(way))
            def _():
                hop_copy(0, stage, way).wait_send()

            @pl.when(hop_exists(way) & edge)
            def _():
                hop_copy(1, stage, way).wait_send()

    for i in range(ring - 1):
        for s in range(slots):

            @pl.when(has_left & (me < ring - 1 - i))
            def _():
                line_copy(0, ring - 1 - i, s).wait_send()

            @pl.when(has_right & (me > i))
            def _():
                line_copy(1, i, s).wait_send()


def solution(mesh):
    shards, ring = mesh.shape["hier"], mesh.shape["col"]

    def on_device(densities, hamiltonian, couplings, gamma, coeff, node_count):
        slots, _, rows, order = densities.shape
        f32, bf16 = jnp.float32, jnp.bfloat16
        vmem = pl.BlockSpec(memory_space=pltpu.VMEM)
        smem = pl.BlockSpec(memory_space=pltpu.SMEM)
        dma = pltpu.SemaphoreType.DMA
        wide = slots + 2 * DEPTH2
        block = (2, rows, order)
        return pl.pallas_call(
            functools.partial(kernel, shards, ring),
            out_shape=jax.ShapeDtypeStruct(densities.shape, f32),
            in_specs=[smem] * 3 + [pl.BlockSpec(memory_space=pltpu.HBM)] * 3,
            out_specs=vmem,
            scratch_shapes=[
                pltpu.VMEM((slots, *block), f32),
                pltpu.VMEM((order, order), f32),
                pltpu.VMEM((2, order, order), f32),
                pltpu.VMEM((2, DEPTH2, *block), f32),
                pltpu.VMEM((2, 2, DEPTH2, *block), f32),
                pltpu.VMEM((2, 2, DEPTH2, *block), f32),
                pltpu.VMEM((2, 2, DEPTH2, *block), f32),
                pltpu.VMEM((slots + 2 * REACH, *block), f32),
                pltpu.VMEM((wide, *block), f32),
                pltpu.VMEM((3 * order, order), bf16),
                pltpu.VMEM((3 * order, order), bf16),
                pltpu.VMEM((wide, 2 * rows, 3 * order), bf16),
                pltpu.VMEM((wide, 2 * rows, 3 * order), bf16),
                pltpu.VMEM((wide, *block), f32),
                pltpu.VMEM((wide, *block), f32),
                pltpu.VMEM((wide, *block), f32),
                pltpu.VMEM((2, slots, *block), f32),
                pltpu.VMEM((2, order, 9 * rows), bf16),
                pltpu.VMEM((2, order, 9 * rows), bf16),
                pltpu.VMEM((slots, *block), f32),
                pltpu.VMEM((slots, 9 * rows, 2 * order), bf16),
                pltpu.VMEM((slots, 9 * rows, 2 * order), bf16),
                pltpu.VMEM((slots, order, 2 * order), f32),
                pltpu.VMEM((slots, *block), f32),
                pltpu.VMEM((ring, slots, rows, 2 * order), f32),
                pltpu.VMEM((ring, slots, rows, 2 * order), f32),
                dma((slots,)),
                dma((slots,)),
                dma((2, 2, 2)),
                dma((2, 2, 2)),
                dma((2, ring, slots)),
                dma((2, ring, slots)),
                dma((3,)),
            ],
            compiler_params=pltpu.CompilerParams(
                collective_id=0, has_side_effects=True, vmem_limit_bytes=67_043_328
            ),
        )(node_count, gamma, coeff, densities, hamiltonian, couplings)

    return jax.shard_map(
        on_device,
        mesh=mesh,
        in_specs=(P("hier", None, "col", None), P(), P(), P(), P(), P()),
        out_specs=P("hier", None, "col", None),
        check_vma=False,
    )
```

```python
import functools

import jax
import jax.numpy as jnp
from jax import lax
from jax.experimental import pallas as pl
from jax.experimental.pallas import tpu as pltpu
from jax.sharding import PartitionSpec as P

DEPTH2 = 2
REACH = 2 * DEPTH2
WINDOW = 4
LAG = 2
OWN_AT = 3
NEAR_AT = 5
FAR_AT = 8
MESH = pl.DeviceIdType.MESH
step_size = 0.2
second = step_size * 0.5 * step_size


def split(value):
    high = value.astype(jnp.bfloat16)
    low = (value - high.astype(jnp.float32)).astype(jnp.bfloat16)
    return high, low


def product(high, low, rhs_high, rhs_low):
    rows = high.shape[0]
    both = jnp.concatenate([high, low], axis=0)
    wide = jnp.dot(both, rhs_high, preferred_element_type=jnp.float32)
    rest = jnp.dot(high, rhs_low, preferred_element_type=jnp.float32)
    return wide[:rows] + (wide[rows:] + rest)


def number(flag):
    return jnp.where(flag, jnp.float32(1), jnp.float32(0))


def kernel(
    shards,
    ring,
    counts,
    gamma,
    coeff,
    x_hbm,
    h_hbm,
    q_hbm,
    out_ref,
    x_ref,
    h_ref,
    q_ref,
    near_out,
    far_out,
    near_in,
    far_in,
    nodes,
    raised,
    right_high,
    right_low,
    mixed_high,
    mixed_low,
    turned,
    drive,
    decay,
    coupled,
    left_high,
    left_low,
    raw_in,
    stack_high,
    stack_low,
    sums,
    own,
    total,
    from_left,
    from_right,
    raw_send,
    raw_recv,
    hop_send,
    hop_recv,
    line_send,
    line_recv,
    load_sem,
):
    slots, _, rows, order = x_hbm.shape
    here = lax.axis_index("hier")
    me = lax.axis_index("col")
    has_lower = here > 0
    has_upper = here < shards - 1
    has_left = me > 0
    has_right = me < ring - 1
    f32 = jnp.float32

    loads = [
        pltpu.make_async_copy(source, place, load_sem.at[i])
        for i, (source, place) in enumerate(((x_hbm, x_ref), (h_hbm, h_ref), (q_hbm, q_ref)))
    ]
    for load in loads:
        load.start()

    barrier = pltpu.get_barrier_semaphore()
    neighbours = (
        (has_left, (here, me - 1)),
        (has_right, (here, me + 1)),
        (has_lower, (here - 1, me)),
        (has_upper, (here + 1, me)),
    )
    greeted = jnp.int32(0)
    for exists, device in neighbours:

        @pl.when(exists)
        def _():
            pl.semaphore_signal(barrier, inc=1, device_id=device, device_id_type=MESH)

        greeted = greeted + exists.astype(jnp.int32)
    pl.semaphore_wait(barrier, greeted)

    edge = (me == 1) | (me == ring - 2)
    end = jnp.where(me == 1, 0, ring - 1)

    def raw_copy(s):
        return pltpu.make_async_remote_copy(
            src_ref=x_hbm.at[s],
            dst_ref=raw_in.at[s],
            send_sem=raw_send.at[s],
            recv_sem=raw_recv.at[s],
            device_id=(here, jnp.where(me == 0, 1, ring - 2)),
            device_id_type=MESH,
        )

    def hop_copy(turn, stage, way):
        if stage == 0:
            first = (x_hbm if turn == 0 else raw_in).at[pl.ds(0, DEPTH2)]
            source = near_out.at[turn] if way == 0 else first
            place = near_in.at[turn, way]
        else:
            source, place = far_out.at[turn, way], far_in.at[turn, way]
        return pltpu.make_async_remote_copy(
            src_ref=source,
            dst_ref=place,
            send_sem=hop_send.at[turn, stage, way],
            recv_sem=hop_recv.at[turn, stage, way],
            device_id=(here + 1, me) if way == 0 else (here - 1, me),
            device_id_type=MESH,
        )

    def hop_exists(way):
        return has_upper if way == 0 else has_lower

    def hop_comes(way):
        return has_lower if way == 0 else has_upper

    @pl.when(has_lower)
    def _():
        hop_copy(0, 0, 1).start()

    @pl.when(jnp.logical_not(has_left & has_right))
    def _():
        for s in range(slots):
            raw_copy(s).start()

    for turn in range(2):
        for way in range(2):

            @pl.when(jnp.logical_not(hop_comes(way)))
            def _():
                near_in[turn, way] = jnp.zeros(near_in.shape[2:], f32)
                far_in[turn, way] = jnp.zeros(far_in.shape[2:], f32)

    offset = jnp.int32(0)
    nodes_held = jnp.int32(0)
    count = jnp.int32(0)
    for i in range(shards):
        held = counts[i]
        nodes_held = nodes_held + held
        offset = offset + jnp.where(here > i, held, 0)
        count = count + jnp.where(here == i, held, 0)
    live_total = nodes_held // DEPTH2 * DEPTH2
    tops = live_total // DEPTH2
    is_count = {c: number(count == c) for c in range(slots // 2, slots + 1)}

    start = offset + count - slots
    margin = REACH + slots

    def levels(k):
        node = start + k
        level = (node + margin) // DEPTH2 - margin // DEPTH2
        return level, node - level * DEPTH2, number((node >= 0) & (node < live_total))

    def root(value):
        return jnp.sqrt(jnp.full((1, order), value, f32))

    zeroth, first, inside, damping = {}, {}, {}, {}
    for k in range(-REACH, slots + REACH):
        zeroth[k], first[k], inside[k] = levels(k)
        damping[k] = zeroth[k].astype(f32) * gamma[0] + first[k].astype(f32) * gamma[1]
    weights = {}
    for k in range(-DEPTH2, slots + DEPTH2):
        base = jnp.maximum(zeroth[k], 0).astype(f32)
        above = first[k].astype(f32)
        ok = number(first[k] + 1 < DEPTH2)
        weights[k, 0] = (
            root(base + 1.0) * (inside[k] * inside[k + DEPTH2]),
            root(base) * (inside[k] * inside[k - DEPTH2]),
        )
        weights[k, 1] = (
            root(above + 1.0) * (inside[k] * inside[k + 1] * ok),
            root(above) * (inside[k] * inside[k - 1]),
        )

    def mixes(array, shift, k, mode):
        stride = DEPTH2 if mode == 0 else 1
        rise, fall = weights[k, mode]
        up, down = k + stride + shift, k - stride + shift
        up_re, up_im = array[up, 0], array[up, 1]
        down_re, down_im = array[down, 0], array[down, 1]
        real, imag = fall * coeff[mode, 0], fall * coeff[mode, 1]
        base_re = rise * up_re + real * down_re
        base_im = rise * up_im + real * down_im
        turn_re, turn_im = imag * down_im, imag * down_re
        plain = (base_re - turn_re, base_im + turn_im)
        conjugate = (base_re + turn_re, base_im - turn_im)
        return plain, conjugate

    def put_mixed(k, a, value):
        for p in range(2):
            high, low = split(value[p])
            at = pl.ds(p * rows, rows), pl.ds(a * order, order)
            mixed_high[(k + DEPTH2,) + at] = high
            mixed_low[(k + DEPTH2,) + at] = low

    def right_product(k, size):
        at = k + DEPTH2
        value = product(
            mixed_high[at : at + size].reshape(size * 2 * rows, 3 * order),
            mixed_low[at : at + size].reshape(size * 2 * rows, 3 * order),
            right_high[...],
            right_low[...],
        )
        return value.reshape(size, 2, rows, order)

    def send_near(turn, state):
        for j in range(DEPTH2):
            for p in range(2):
                value = None
                for c in is_count:
                    term = is_count[c] * state[c - 1 - j, p]
                    value = term if value is None else value + term
                near_out[turn, j, p] = value

        @pl.when(has_upper)
        def _():
            hop_copy(turn, 0, 0).start()

    loads[0].wait()
    send_near(0, x_ref)

    for load in loads[1:]:
        load.wait()

    mine = pl.ds(pl.multiple_of(me * rows, rows), rows)
    for a in range(3):
        high, low = split(h_ref[...] if a == 0 else q_ref[a - 1])
        right_high[a * order : (a + 1) * order] = high
        right_low[a * order : (a + 1) * order] = low

    def left_factors(turn, lines):
        factors = [h_ref[lines, :], q_ref[0, lines, :], q_ref[1, lines, :]]
        high, low = split(jnp.concatenate(factors, axis=0))
        twice = []
        for a in range(3):
            at = slice(a * order, (a + 1) * order)
            value = product(high, low, right_high[at], right_low[at])
            twice.append([value[b * rows : (b + 1) * rows] for b in range(3)])
        parts = factors + [
            -second * twice[0][0],
            -second * (twice[0][1] + twice[1][0]),
            -second * (twice[0][2] + twice[2][0]),
            -second * (twice[1][2] + twice[2][1]),
            -second * twice[1][1],
            -second * twice[2][2],
        ]
        high, low = split(jnp.concatenate(parts, axis=0).T)
        left_high[turn] = high
        left_low[turn] = low

    left_factors(0, mine)

    @pl.when(edge)
    def _():
        left_factors(1, pl.ds(pl.multiple_of(end * rows, rows), rows))

    def couple():
        here_nodes = nodes[REACH : REACH + slots]
        high, low = split(here_nodes.reshape(slots * 2 * rows, order))
        for mode in range(2):
            at = slice((mode + 1) * order, (mode + 2) * order)
            value = product(high, low, right_high[at], right_low[at])
            coupled[mode] = value.reshape(slots, 2, rows, order)

    def chosen(term_of):
        value = None
        for c in is_count:
            term = term_of(c)
            if term is not None:
                term = is_count[c] * term
                value = term if value is None else value + term
        return value

    def below(turn, d, p):
        if d > REACH:
            return None
        if d > DEPTH2:
            return far_in[turn, 0, d - 1 - DEPTH2, p]
        return near_in[turn, 0, d - 1, p]

    def gather_near(turn, state):
        @pl.when(has_lower)
        def _():
            hop_copy(turn, 0, 0).wait_recv()

        for k in range(slots):
            for p in range(2):

                def held(c):
                    at = k + c - slots
                    return state[at, p] if at >= 0 else below(turn, -at, p)

                nodes[REACH + k, p] = chosen(held) * inside[k]
        for j in range(DEPTH2):
            for p in range(2):
                far_out[turn, 0, j, p] = nodes[REACH + slots - 1 - DEPTH2 - j, p]

        @pl.when(has_upper)
        def _():
            hop_copy(turn, 1, 0).start()
            hop_copy(turn, 0, 1).wait_recv()

        for j in range(DEPTH2):
            for p in range(2):
                nodes[REACH + slots + j, p] = near_in[turn, 1, j, p] * inside[slots + j]
                at = DEPTH2 + j

                def next_node(c):
                    return state[at, p] if at < c else near_in[turn, 1, at - c, p]

                far_out[turn, 1, j, p] = chosen(next_node)

        @pl.when(has_lower)
        def _():
            hop_copy(turn, 1, 1).start()

    def gather_below(turn):
        @pl.when(has_lower)
        def _():
            hop_copy(turn, 1, 0).wait_recv()

        for d in range(1, REACH + 1):
            for p in range(2):
                value = chosen(lambda c: below(turn, d + slots - c, p))
                nodes[REACH - d, p] = value * inside[-d]

    def gather_above(turn):
        @pl.when(has_upper)
        def _():
            hop_copy(turn, 1, 1).wait_recv()

        for j in range(DEPTH2):
            for p in range(2):
                at = slots + DEPTH2 + j
                nodes[REACH + at, p] = far_in[turn, 1, j, p] * inside[at]

    wide = range(-DEPTH2, slots + DEPTH2)

    def put_stack(s, a, value):
        for p in range(2):
            high, low = split(value[p])
            at = pl.ds(a * rows, rows), pl.ds(p * order, order)
            stack_high[(s,) + at] = high
            stack_low[(s,) + at] = low

    def mix_nodes(places):
        for k in places:
            plain, conjugate = mixes(nodes, REACH, k, 0)
            for p in range(2):
                raised[k + DEPTH2, p] = plain[p]
            put_mixed(k, 0, (nodes[k + REACH, 0], nodes[k + REACH, 1]))
            put_mixed(k, 1, conjugate)
            plain, conjugate = mixes(nodes, REACH, k, 1)
            put_mixed(k, 2, conjugate)
            if 0 <= k < slots:
                put_stack(k, 5, plain)

    def turn_nodes(first, size):
        turned[first + DEPTH2 : first + DEPTH2 + size] = right_product(first, size)
        for k in range(first, first + size):
            at = k + DEPTH2
            beta = second * damping[k] - step_size
            x_re, x_im = nodes[k + REACH, 0], nodes[k + REACH, 1]
            drive[at, 0] = (2 * second) * turned[at, 0] - beta * x_im
            drive[at, 1] = (2 * second) * turned[at, 1] + beta * x_re

    half = slots // 2
    gather_near(0, x_ref)
    couple()
    gather_below(0)
    mix_nodes(range(-DEPTH2, half + DEPTH2))
    turn_nodes(-DEPTH2, half + 2 * DEPTH2)

    def panel(q):
        return pl.ds(pl.multiple_of(q * rows, rows), rows)

    def line_copy(way, q, s):
        place = from_left if way == 0 else from_right
        return pltpu.make_async_remote_copy(
            src_ref=sums.at[s, panel(q), :],
            dst_ref=place.at[q, s],
            send_sem=line_send.at[way, q, s],
            recv_sem=line_recv.at[way, q, s],
            device_id=(here, me + 1) if way == 0 else (here, me - 1),
            device_id_type=MESH,
        )

    blocks = (ring - 2) * slots

    early = (ring - 2) * half

    def which(j):
        group = j // early
        rest = j - group * early
        return rest // half, group * half + lax.rem(rest, half)

    def end_copy(way, j):
        q, s = which(j)
        return line_copy(way, ring - 1 - q if way == 0 else q, s)

    def feed_one(way, j):
        @pl.when((j >= WINDOW) & (j < blocks + WINDOW))
        def _():
            end_copy(way, j - WINDOW).wait_send()

        @pl.when(j < blocks)
        def _():
            end_copy(way, j).start()

    def feed(j):
        for way, inner in ((0, has_left), (1, has_right)):

            @pl.when(jnp.logical_not(inner))
            def _():
                feed_one(way, jnp.int32(j))

    def fill_stack(s):
        at = s + DEPTH2
        tilt = second * damping[s]
        x_re, x_im = nodes[s + REACH, 0], nodes[s + REACH, 1]
        put_stack(s, 0, (drive[at, 0] - tilt * x_im, drive[at, 1] + tilt * x_re))
        top = zeroth[s].astype(f32)
        lift = (
            number(zeroth[s] + 1 < tops) * (top + 1.0) - top,
            number(first[s] + 1 < DEPTH2) * (first[s].astype(f32) + 1.0) - first[s].astype(f32),
        )
        for mode in range(2):
            plain, _ = mixes(drive, DEPTH2, s, mode)
            if mode == 0:
                linked = raised[at, 0], raised[at, 1]
            else:
                linked, _ = mixes(nodes, REACH, s, 1)
            turn = 2 * second * coeff[mode, 1] * lift[mode]
            put_stack(
                s,
                mode + 1,
                (
                    plain[0] - tilt * linked[1] - turn * coupled[mode, s, 1],
                    plain[1] + tilt * linked[0] + turn * coupled[mode, s, 0],
                ),
            )
        put_stack(s, 3, (x_re, x_im))
        put_stack(s, 4, (raised[at, 0], raised[at, 1]))
        plain, _ = mixes(raised, DEPTH2, s, 1)
        put_stack(s, 6, plain)
        plain, _ = mixes(raised, DEPTH2, s, 0)
        put_stack(s, 7, plain)
        real, imag = coeff[1, 0], coeff[1, 1]
        put_stack(s, 8, (real * x_re - imag * x_im, real * x_im + imag * x_re))

    def contribute(s):
        fill_stack(s)
        sums[s] = product(left_high[0], left_low[0], stack_high[s], stack_low[s])

    fed = min(WINDOW, early)
    for s in range(half):
        contribute(s)
        for j in range(fed if s == half - 1 else s + 1):
            if j >= s:
                feed(j)
    gather_above(0)
    mix_nodes(range(half + DEPTH2, slots + DEPTH2))
    turn_nodes(half + DEPTH2, half)
    for s in range(half, slots):
        contribute(s)

    @pl.when(edge)
    def _():
        for s in range(slots):
            raw_copy(s).wait_recv()

        @pl.when(has_lower)
        def _():
            hop_copy(1, 0, 1).start()

        send_near(1, raw_in)

    def own_terms():
        for k in wide:
            at = k + DEPTH2
            x_re, x_im = nodes[k + REACH, 0], nodes[k + REACH, 1]
            decay[at, 0] = (second * damping[k]) * x_im - second * turned[at, 0]
            decay[at, 1] = -(second * damping[k]) * x_re - second * turned[at, 1]
        for s in range(slots):
            put_mixed(s, 0, (decay[s + DEPTH2, 0], decay[s + DEPTH2, 1]))
            for mode in range(2):
                _, conjugate = mixes(decay, DEPTH2, s, mode)
                put_mixed(s, mode + 1, conjugate)
        own[...] = right_product(0, slots)
        for s in range(slots):
            at = s + DEPTH2
            rate = damping[s]
            keep = 1.0 - step_size * rate + second * rate * rate
            beta = step_size - second * rate
            own_re = own[s, 0] + keep * nodes[s + REACH, 0] - beta * turned[at, 1]
            own_im = own[s, 1] + keep * nodes[s + REACH, 1] + beta * turned[at, 0]
            total[s, 0] = own_re + sums[s, mine, :order]
            total[s, 1] = own_im + sums[s, mine, order:]

    def pass_on(way, t):
        place = from_left if way == 0 else from_right
        passed = me if way == 0 else ring - 1 - me
        j = t - LAG * passed
        inner = (passed > 0) & (j >= 0) & (j < blocks)
        step, s = which(jnp.maximum(j, 0))
        q = ring - 1 - step if way == 0 else step

        @pl.when(inner & (step < ring - 1 - passed))
        def _():
            line = panel(q)
            line_copy(way, q, s).wait_recv()
            sums[s, line, :] = sums[s, line, :] + place[q, s]
            line_copy(way, q, s).start()

        @pl.when(inner & (step == ring - 1 - passed))
        def _():
            line_copy(way, q, s).wait_recv()
            total[s, 0] = total[s, 0] + place[q, s, :, :order]
            total[s, 1] = total[s, 1] + place[q, s, :, order:]

    def advance(t, carry):
        for way, passed in ((0, me), (1, ring - 1 - me)):

            @pl.when((passed == 0) & (t >= fed))
            def _():
                feed_one(way, t)

        for way in range(2):
            pass_on(way, t)
        return carry

    def act(s):
        fill_stack(s)
        value = product(left_high[1, mine, :], left_low[1, mine, :], stack_high[s], stack_low[s])
        total[s, 0] = total[s, 0] + value[:, :order]
        total[s, 1] = total[s, 1] + value[:, order:]

    def extra_near():
        gather_near(1, raw_in)
        couple()

    def extra_far():
        gather_below(1)
        gather_above(1)
        mix_nodes(wide)

    extras = (
        (NEAR_AT, extra_near),
        (FAR_AT, extra_far),
        (FAR_AT + 1, functools.partial(turn_nodes, -DEPTH2, half + DEPTH2)),
        (FAR_AT + 2, functools.partial(turn_nodes, half, half + DEPTH2)),
        (FAR_AT + 3, lambda: [act(s) for s in range(slots // 2)]),
        (FAR_AT + 4, lambda: [act(s) for s in range(slots // 2, slots)]),
    )
    lax.fori_loop(0, OWN_AT, advance, 0)
    own_terms()
    begin = OWN_AT
    for at, extra in extras:
        lax.fori_loop(begin, at, advance, 0)
        begin = at

        @pl.when(edge)
        def _():
            extra()

    lax.fori_loop(begin, blocks + max(WINDOW, LAG * (ring - 1)), advance, 0)
    for s in range(slots):
        alive = number((offset + s < live_total) & (s < count))
        for p in range(2):
            value = chosen(lambda c: total[s + slots - c, p] if s < c else None)
            out_ref[s, p] = alive * value + (1.0 - alive) * x_ref[s, p]

    @pl.when(jnp.logical_not(has_left & has_right))
    def _():
        for s in range(slots):
            raw_copy(s).wait_send()

    for stage in range(2):
        for way in range(2):

            @pl.when(hop_exists(way))
            def _():
                hop_copy(0, stage, way).wait_send()

            @pl.when(hop_exists(way) & edge)
            def _():
                hop_copy(1, stage, way).wait_send()

    for i in range(ring - 1):
        for s in range(slots):

            @pl.when(has_left & (me < ring - 1 - i))
            def _():
                line_copy(0, ring - 1 - i, s).wait_send()

            @pl.when(has_right & (me > i))
            def _():
                line_copy(1, i, s).wait_send()


def solution(mesh):
    shards, ring = mesh.shape["hier"], mesh.shape["col"]

    def on_device(densities, hamiltonian, couplings, gamma, coeff, node_count):
        slots, _, rows, order = densities.shape
        f32, bf16 = jnp.float32, jnp.bfloat16
        vmem = pl.BlockSpec(memory_space=pltpu.VMEM)
        smem = pl.BlockSpec(memory_space=pltpu.SMEM)
        dma = pltpu.SemaphoreType.DMA
        wide = slots + 2 * DEPTH2
        block = (2, rows, order)
        return pl.pallas_call(
            functools.partial(kernel, shards, ring),
            out_shape=jax.ShapeDtypeStruct(densities.shape, f32),
            in_specs=[smem] * 3 + [pl.BlockSpec(memory_space=pltpu.HBM)] * 3,
            out_specs=vmem,
            scratch_shapes=[
                pltpu.VMEM((slots, *block), f32),
                pltpu.VMEM((order, order), f32),
                pltpu.VMEM((2, order, order), f32),
                pltpu.VMEM((2, DEPTH2, *block), f32),
                pltpu.VMEM((2, 2, DEPTH2, *block), f32),
                pltpu.VMEM((2, 2, DEPTH2, *block), f32),
                pltpu.VMEM((2, 2, DEPTH2, *block), f32),
                pltpu.VMEM((slots + 2 * REACH, *block), f32),
                pltpu.VMEM((wide, *block), f32),
                pltpu.VMEM((3 * order, order), bf16),
                pltpu.VMEM((3 * order, order), bf16),
                pltpu.VMEM((wide, 2 * rows, 3 * order), bf16),
                pltpu.VMEM((wide, 2 * rows, 3 * order), bf16),
                pltpu.VMEM((wide, *block), f32),
                pltpu.VMEM((wide, *block), f32),
                pltpu.VMEM((wide, *block), f32),
                pltpu.VMEM((2, slots, *block), f32),
                pltpu.VMEM((2, order, 9 * rows), bf16),
                pltpu.VMEM((2, order, 9 * rows), bf16),
                pltpu.VMEM((slots, *block), f32),
                pltpu.VMEM((slots, 9 * rows, 2 * order), bf16),
                pltpu.VMEM((slots, 9 * rows, 2 * order), bf16),
                pltpu.VMEM((slots, order, 2 * order), f32),
                pltpu.VMEM((slots, *block), f32),
                pltpu.VMEM((slots, *block), f32),
                pltpu.VMEM((ring, slots, rows, 2 * order), f32),
                pltpu.VMEM((ring, slots, rows, 2 * order), f32),
                dma((slots,)),
                dma((slots,)),
                dma((2, 2, 2)),
                dma((2, 2, 2)),
                dma((2, ring, slots)),
                dma((2, ring, slots)),
                dma((3,)),
            ],
            compiler_params=pltpu.CompilerParams(
                collective_id=0, has_side_effects=True, vmem_limit_bytes=67_043_328
            ),
        )(node_count, gamma, coeff, densities, hamiltonian, couplings)

    return jax.shard_map(
        on_device,
        mesh=mesh,
        in_specs=(P("hier", None, "col", None), P(), P(), P(), P(), P()),
        out_specs=P("hier", None, "col", None),
        check_vma=False,
    )
```

```python
import functools

import jax
import jax.numpy as jnp
from jax import lax
from jax.experimental import pallas as pl
from jax.experimental.pallas import tpu as pltpu
from jax.sharding import PartitionSpec as P

DEPTH2 = 2
REACH = 2 * DEPTH2
WINDOW = 4
LAG = 2
LATE_AT = 3
NEAR_AT = 6
FAR_AT = 9
MESH = pl.DeviceIdType.MESH
step_size = 0.2
second = step_size * 0.5 * step_size


def split(value):
    high = value.astype(jnp.bfloat16)
    low = (value - high.astype(jnp.float32)).astype(jnp.bfloat16)
    return high, low


def product(high, low, rhs_high, rhs_low):
    rows = high.shape[0]
    both = jnp.concatenate([high, low], axis=0)
    wide = jnp.dot(both, rhs_high, preferred_element_type=jnp.float32)
    rest = jnp.dot(high, rhs_low, preferred_element_type=jnp.float32)
    return wide[:rows] + (wide[rows:] + rest)


def number(flag):
    return jnp.where(flag, jnp.float32(1), jnp.float32(0))


def kernel(
    shards,
    ring,
    counts,
    gamma,
    coeff,
    x_hbm,
    h_hbm,
    q_hbm,
    out_ref,
    x_ref,
    h_ref,
    q_ref,
    near_out,
    far_out,
    near_in,
    far_in,
    nodes,
    raised,
    right_high,
    right_low,
    mixed_high,
    mixed_low,
    turned,
    drive,
    decay,
    coupled,
    left_high,
    left_low,
    raw_in,
    stack_high,
    stack_low,
    sums,
    own,
    total,
    from_left,
    from_right,
    raw_send,
    raw_recv,
    hop_send,
    hop_recv,
    line_send,
    line_recv,
    load_sem,
):
    slots, _, rows, order = x_hbm.shape
    here = lax.axis_index("hier")
    me = lax.axis_index("col")
    has_lower = here > 0
    has_upper = here < shards - 1
    has_left = me > 0
    has_right = me < ring - 1
    f32 = jnp.float32

    loads = [
        pltpu.make_async_copy(source, place, load_sem.at[i])
        for i, (source, place) in enumerate(((x_hbm, x_ref), (h_hbm, h_ref), (q_hbm, q_ref)))
    ]
    for load in loads:
        load.start()

    barrier = pltpu.get_barrier_semaphore()
    neighbours = (
        (has_left, (here, me - 1)),
        (has_right, (here, me + 1)),
        (has_lower, (here - 1, me)),
        (has_upper, (here + 1, me)),
    )
    greeted = jnp.int32(0)
    for exists, device in neighbours:

        @pl.when(exists)
        def _():
            pl.semaphore_signal(barrier, inc=1, device_id=device, device_id_type=MESH)

        greeted = greeted + exists.astype(jnp.int32)
    pl.semaphore_wait(barrier, greeted)

    edge = (me == 1) | (me == ring - 2)
    end = jnp.where(me == 1, 0, ring - 1)

    def raw_copy(s):
        return pltpu.make_async_remote_copy(
            src_ref=x_hbm.at[s],
            dst_ref=raw_in.at[s],
            send_sem=raw_send.at[s],
            recv_sem=raw_recv.at[s],
            device_id=(here, jnp.where(me == 0, 1, ring - 2)),
            device_id_type=MESH,
        )

    def hop_copy(turn, stage, way):
        if stage == 0:
            first = (x_hbm if turn == 0 else raw_in).at[pl.ds(0, DEPTH2)]
            source = near_out.at[turn] if way == 0 else first
            place = near_in.at[turn, way]
        else:
            source, place = far_out.at[turn, way], far_in.at[turn, way]
        return pltpu.make_async_remote_copy(
            src_ref=source,
            dst_ref=place,
            send_sem=hop_send.at[turn, stage, way],
            recv_sem=hop_recv.at[turn, stage, way],
            device_id=(here + 1, me) if way == 0 else (here - 1, me),
            device_id_type=MESH,
        )

    def hop_exists(way):
        return has_upper if way == 0 else has_lower

    def hop_comes(way):
        return has_lower if way == 0 else has_upper

    @pl.when(has_lower)
    def _():
        hop_copy(0, 0, 1).start()

    @pl.when(jnp.logical_not(has_left & has_right))
    def _():
        for s in range(slots):
            raw_copy(s).start()

    for turn in range(2):
        for way in range(2):

            @pl.when(jnp.logical_not(hop_comes(way)))
            def _():
                near_in[turn, way] = jnp.zeros(near_in.shape[2:], f32)
                far_in[turn, way] = jnp.zeros(far_in.shape[2:], f32)

    offset = jnp.int32(0)
    nodes_held = jnp.int32(0)
    count = jnp.int32(0)
    for i in range(shards):
        held = counts[i]
        nodes_held = nodes_held + held
        offset = offset + jnp.where(here > i, held, 0)
        count = count + jnp.where(here == i, held, 0)
    live_total = nodes_held // DEPTH2 * DEPTH2
    tops = live_total // DEPTH2
    is_count = {c: number(count == c) for c in range(slots // 2, slots + 1)}

    start = offset + count - slots
    margin = REACH + slots

    def levels(k):
        node = start + k
        level = (node + margin) // DEPTH2 - margin // DEPTH2
        return level, node - level * DEPTH2, number((node >= 0) & (node < live_total))

    def root(value):
        return jnp.sqrt(jnp.full((1, order), value, f32))

    zeroth, first, inside, damping = {}, {}, {}, {}
    for k in range(-REACH, slots + REACH):
        zeroth[k], first[k], inside[k] = levels(k)
        damping[k] = zeroth[k].astype(f32) * gamma[0] + first[k].astype(f32) * gamma[1]
    weights = {}
    for k in range(-DEPTH2, slots + DEPTH2):
        base = jnp.maximum(zeroth[k], 0).astype(f32)
        above = first[k].astype(f32)
        ok = number(first[k] + 1 < DEPTH2)
        weights[k, 0] = (
            root(base + 1.0) * (inside[k] * inside[k + DEPTH2]),
            root(base) * (inside[k] * inside[k - DEPTH2]),
        )
        weights[k, 1] = (
            root(above + 1.0) * (inside[k] * inside[k + 1] * ok),
            root(above) * (inside[k] * inside[k - 1]),
        )

    def mixes(array, shift, k, mode):
        stride = DEPTH2 if mode == 0 else 1
        rise, fall = weights[k, mode]
        up, down = k + stride + shift, k - stride + shift
        up_re, up_im = array[up, 0], array[up, 1]
        down_re, down_im = array[down, 0], array[down, 1]
        real, imag = fall * coeff[mode, 0], fall * coeff[mode, 1]
        base_re = rise * up_re + real * down_re
        base_im = rise * up_im + real * down_im
        turn_re, turn_im = imag * down_im, imag * down_re
        plain = (base_re - turn_re, base_im + turn_im)
        conjugate = (base_re + turn_re, base_im - turn_im)
        return plain, conjugate

    def put_mixed(k, a, value):
        for p in range(2):
            high, low = split(value[p])
            at = pl.ds(p * rows, rows), pl.ds(a * order, order)
            mixed_high[(k + DEPTH2,) + at] = high
            mixed_low[(k + DEPTH2,) + at] = low

    def right_product(k, size):
        at = k + DEPTH2
        value = product(
            mixed_high[at : at + size].reshape(size * 2 * rows, 3 * order),
            mixed_low[at : at + size].reshape(size * 2 * rows, 3 * order),
            right_high[...],
            right_low[...],
        )
        return value.reshape(size, 2, rows, order)

    def send_near(turn, state):
        for j in range(DEPTH2):
            for p in range(2):
                value = None
                for c in is_count:
                    term = is_count[c] * state[c - 1 - j, p]
                    value = term if value is None else value + term
                near_out[turn, j, p] = value

        @pl.when(has_upper)
        def _():
            hop_copy(turn, 0, 0).start()

    loads[0].wait()
    send_near(0, x_ref)

    for load in loads[1:]:
        load.wait()

    mine = pl.ds(pl.multiple_of(me * rows, rows), rows)
    for a in range(3):
        high, low = split(h_ref[...] if a == 0 else q_ref[a - 1])
        right_high[a * order : (a + 1) * order] = high
        right_low[a * order : (a + 1) * order] = low

    def left_factors(turn, lines):
        factors = [h_ref[lines, :], q_ref[0, lines, :], q_ref[1, lines, :]]
        high, low = split(jnp.concatenate(factors, axis=0))
        twice = []
        for a in range(3):
            at = slice(a * order, (a + 1) * order)
            value = product(high, low, right_high[at], right_low[at])
            twice.append([value[b * rows : (b + 1) * rows] for b in range(3)])
        parts = factors + [
            -second * twice[0][0],
            -second * (twice[0][1] + twice[1][0]),
            -second * (twice[0][2] + twice[2][0]),
            -second * (twice[1][2] + twice[2][1]),
            -second * twice[1][1],
            -second * twice[2][2],
        ]
        high, low = split(jnp.concatenate(parts, axis=0).T)
        left_high[turn] = high
        left_low[turn] = low

    left_factors(0, mine)

    @pl.when(edge)
    def _():
        left_factors(1, pl.ds(pl.multiple_of(end * rows, rows), rows))

    def couple():
        here_nodes = nodes[REACH : REACH + slots]
        high, low = split(here_nodes.reshape(slots * 2 * rows, order))
        for mode in range(2):
            at = slice((mode + 1) * order, (mode + 2) * order)
            value = product(high, low, right_high[at], right_low[at])
            coupled[mode] = value.reshape(slots, 2, rows, order)

    def chosen(term_of):
        value = None
        for c in is_count:
            term = term_of(c)
            if term is not None:
                term = is_count[c] * term
                value = term if value is None else value + term
        return value

    def below(turn, d, p):
        if d > REACH:
            return None
        if d > DEPTH2:
            return far_in[turn, 0, d - 1 - DEPTH2, p]
        return near_in[turn, 0, d - 1, p]

    def gather_near(turn, state):
        @pl.when(has_lower)
        def _():
            hop_copy(turn, 0, 0).wait_recv()

        for k in range(slots):
            for p in range(2):

                def held(c):
                    at = k + c - slots
                    return state[at, p] if at >= 0 else below(turn, -at, p)

                nodes[REACH + k, p] = chosen(held) * inside[k]
        for j in range(DEPTH2):
            for p in range(2):
                far_out[turn, 0, j, p] = nodes[REACH + slots - 1 - DEPTH2 - j, p]

        @pl.when(has_upper)
        def _():
            hop_copy(turn, 1, 0).start()
            hop_copy(turn, 0, 1).wait_recv()

        for j in range(DEPTH2):
            for p in range(2):
                nodes[REACH + slots + j, p] = near_in[turn, 1, j, p] * inside[slots + j]
                at = DEPTH2 + j

                def next_node(c):
                    return state[at, p] if at < c else near_in[turn, 1, at - c, p]

                far_out[turn, 1, j, p] = chosen(next_node)

        @pl.when(has_lower)
        def _():
            hop_copy(turn, 1, 1).start()

    def gather_below(turn):
        @pl.when(has_lower)
        def _():
            hop_copy(turn, 1, 0).wait_recv()

        for d in range(1, REACH + 1):
            for p in range(2):
                value = chosen(lambda c: below(turn, d + slots - c, p))
                nodes[REACH - d, p] = value * inside[-d]

    def gather_above(turn):
        @pl.when(has_upper)
        def _():
            hop_copy(turn, 1, 1).wait_recv()

        for j in range(DEPTH2):
            for p in range(2):
                at = slots + DEPTH2 + j
                nodes[REACH + at, p] = far_in[turn, 1, j, p] * inside[at]

    wide = range(-DEPTH2, slots + DEPTH2)

    def put_stack(s, a, value):
        for p in range(2):
            high, low = split(value[p])
            at = pl.ds(a * rows, rows), pl.ds(p * order, order)
            stack_high[(s,) + at] = high
            stack_low[(s,) + at] = low

    def mix_nodes(places):
        for k in places:
            plain, conjugate = mixes(nodes, REACH, k, 0)
            for p in range(2):
                raised[k + DEPTH2, p] = plain[p]
            put_mixed(k, 0, (nodes[k + REACH, 0], nodes[k + REACH, 1]))
            put_mixed(k, 1, conjugate)
            plain, conjugate = mixes(nodes, REACH, k, 1)
            put_mixed(k, 2, conjugate)
            if 0 <= k < slots:
                put_stack(k, 5, plain)

    def turn_nodes(first, size):
        turned[first + DEPTH2 : first + DEPTH2 + size] = right_product(first, size)
        for k in range(first, first + size):
            at = k + DEPTH2
            beta = second * damping[k] - step_size
            x_re, x_im = nodes[k + REACH, 0], nodes[k + REACH, 1]
            drive[at, 0] = (2 * second) * turned[at, 0] - beta * x_im
            drive[at, 1] = (2 * second) * turned[at, 1] + beta * x_re

    half = slots // 2
    gather_near(0, x_ref)
    couple()
    mix_nodes(range(half, slots))
    turn_nodes(half, slots - half)
    gather_below(0)
    mix_nodes(range(-DEPTH2, half))
    turn_nodes(-DEPTH2, half + DEPTH2)

    def panel(q):
        return pl.ds(pl.multiple_of(q * rows, rows), rows)

    def line_copy(way, q, s):
        place = from_left if way == 0 else from_right
        return pltpu.make_async_remote_copy(
            src_ref=sums.at[s, panel(q), :],
            dst_ref=place.at[q, s],
            send_sem=line_send.at[way, q, s],
            recv_sem=line_recv.at[way, q, s],
            device_id=(here, me + 1) if way == 0 else (here, me - 1),
            device_id_type=MESH,
        )

    blocks = (ring - 2) * slots

    early = (ring - 2) * half

    def which(j):
        group = j // early
        rest = j - group * early
        return rest // half, group * half + lax.rem(rest, half)

    def end_copy(way, j):
        q, s = which(j)
        return line_copy(way, ring - 1 - q if way == 0 else q, s)

    def feed_one(way, j):
        @pl.when((j >= WINDOW) & (j < blocks + WINDOW))
        def _():
            end_copy(way, j - WINDOW).wait_send()

        @pl.when(j < blocks)
        def _():
            end_copy(way, j).start()

    def feed(j):
        for way, inner in ((0, has_left), (1, has_right)):

            @pl.when(jnp.logical_not(inner))
            def _():
                feed_one(way, jnp.int32(j))

    def fill_stack(s):
        at = s + DEPTH2
        tilt = second * damping[s]
        x_re, x_im = nodes[s + REACH, 0], nodes[s + REACH, 1]
        put_stack(s, 0, (drive[at, 0] - tilt * x_im, drive[at, 1] + tilt * x_re))
        top = zeroth[s].astype(f32)
        lift = (
            number(zeroth[s] + 1 < tops) * (top + 1.0) - top,
            number(first[s] + 1 < DEPTH2) * (first[s].astype(f32) + 1.0) - first[s].astype(f32),
        )
        for mode in range(2):
            plain, _ = mixes(drive, DEPTH2, s, mode)
            if mode == 0:
                linked = raised[at, 0], raised[at, 1]
            else:
                linked, _ = mixes(nodes, REACH, s, 1)
            turn = 2 * second * coeff[mode, 1] * lift[mode]
            put_stack(
                s,
                mode + 1,
                (
                    plain[0] - tilt * linked[1] - turn * coupled[mode, s, 1],
                    plain[1] + tilt * linked[0] + turn * coupled[mode, s, 0],
                ),
            )
        put_stack(s, 3, (x_re, x_im))
        put_stack(s, 4, (raised[at, 0], raised[at, 1]))
        plain, _ = mixes(raised, DEPTH2, s, 1)
        put_stack(s, 6, plain)
        plain, _ = mixes(raised, DEPTH2, s, 0)
        put_stack(s, 7, plain)
        real, imag = coeff[1, 0], coeff[1, 1]
        put_stack(s, 8, (real * x_re - imag * x_im, real * x_im + imag * x_re))

    def contribute(s):
        fill_stack(s)
        sums[s] = product(left_high[0], left_low[0], stack_high[s], stack_low[s])

    fed = min(WINDOW, early)
    for s in range(half):
        contribute(s)
        for j in range(fed if s == half - 1 else s + 1):
            if j >= s:
                feed(j)
    def late_turn():
        gather_above(0)
        mix_nodes(range(slots, slots + DEPTH2))
        turn_nodes(slots, DEPTH2)
        contribute(half)

    def late_rest():
        for s in range(half + 1, slots):
            contribute(s)

    @pl.when(edge)
    def _():
        for s in range(slots):
            raw_copy(s).wait_recv()

        @pl.when(has_lower)
        def _():
            hop_copy(1, 0, 1).start()

        send_near(1, raw_in)

    def own_terms():
        for k in wide:
            at = k + DEPTH2
            x_re, x_im = nodes[k + REACH, 0], nodes[k + REACH, 1]
            decay[at, 0] = (second * damping[k]) * x_im - second * turned[at, 0]
            decay[at, 1] = -(second * damping[k]) * x_re - second * turned[at, 1]
        for s in range(slots):
            put_mixed(s, 0, (decay[s + DEPTH2, 0], decay[s + DEPTH2, 1]))
            for mode in range(2):
                _, conjugate = mixes(decay, DEPTH2, s, mode)
                put_mixed(s, mode + 1, conjugate)
        own[...] = right_product(0, slots)
        for s in range(slots):
            at = s + DEPTH2
            rate = damping[s]
            keep = 1.0 - step_size * rate + second * rate * rate
            beta = step_size - second * rate
            own_re = own[s, 0] + keep * nodes[s + REACH, 0] - beta * turned[at, 1]
            own_im = own[s, 1] + keep * nodes[s + REACH, 1] + beta * turned[at, 0]
            total[s, 0] = own_re + sums[s, mine, :order]
            total[s, 1] = own_im + sums[s, mine, order:]

    def pass_on(way, t):
        place = from_left if way == 0 else from_right
        passed = me if way == 0 else ring - 1 - me
        j = t - LAG * passed
        inner = (passed > 0) & (j >= 0) & (j < blocks)
        step, s = which(jnp.maximum(j, 0))
        q = ring - 1 - step if way == 0 else step

        @pl.when(inner & (step < ring - 1 - passed))
        def _():
            line = panel(q)
            line_copy(way, q, s).wait_recv()
            sums[s, line, :] = sums[s, line, :] + place[q, s]
            line_copy(way, q, s).start()

        @pl.when(inner & (step == ring - 1 - passed))
        def _():
            line_copy(way, q, s).wait_recv()
            total[s, 0] = total[s, 0] + place[q, s, :, :order]
            total[s, 1] = total[s, 1] + place[q, s, :, order:]

    def advance(t, carry):
        for way, passed in ((0, me), (1, ring - 1 - me)):

            @pl.when((passed == 0) & (t >= fed))
            def _():
                feed_one(way, t)

        for way in range(2):
            pass_on(way, t)
        return carry

    def act(s):
        fill_stack(s)
        value = product(left_high[1, mine, :], left_low[1, mine, :], stack_high[s], stack_low[s])
        total[s, 0] = total[s, 0] + value[:, :order]
        total[s, 1] = total[s, 1] + value[:, order:]

    def extra_near():
        gather_near(1, raw_in)
        couple()

    def extra_far():
        gather_below(1)
        gather_above(1)
        mix_nodes(wide)

    extras = (
        (NEAR_AT, extra_near),
        (FAR_AT, extra_far),
        (FAR_AT + 1, functools.partial(turn_nodes, -DEPTH2, half + DEPTH2)),
        (FAR_AT + 2, functools.partial(turn_nodes, half, half + DEPTH2)),
        (FAR_AT + 3, lambda: [act(s) for s in range(slots // 2)]),
        (FAR_AT + 4, lambda: [act(s) for s in range(slots // 2, slots)]),
    )
    begin = 0
    for at, stage in ((LATE_AT, late_turn), (LATE_AT + 1, late_rest), (LATE_AT + 2, own_terms)):
        lax.fori_loop(begin, at, advance, 0)
        begin = at
        stage()
    for at, extra in extras:
        lax.fori_loop(begin, at, advance, 0)
        begin = at

        @pl.when(edge)
        def _():
            extra()

    lax.fori_loop(begin, blocks + max(WINDOW, LAG * (ring - 1)), advance, 0)
    for s in range(slots):
        alive = number((offset + s < live_total) & (s < count))
        for p in range(2):
            value = chosen(lambda c: total[s + slots - c, p] if s < c else None)
            out_ref[s, p] = alive * value + (1.0 - alive) * x_ref[s, p]

    @pl.when(jnp.logical_not(has_left & has_right))
    def _():
        for s in range(slots):
            raw_copy(s).wait_send()

    for stage in range(2):
        for way in range(2):

            @pl.when(hop_exists(way))
            def _():
                hop_copy(0, stage, way).wait_send()

            @pl.when(hop_exists(way) & edge)
            def _():
                hop_copy(1, stage, way).wait_send()

    for i in range(ring - 1):
        for s in range(slots):

            @pl.when(has_left & (me < ring - 1 - i))
            def _():
                line_copy(0, ring - 1 - i, s).wait_send()

            @pl.when(has_right & (me > i))
            def _():
                line_copy(1, i, s).wait_send()


def solution(mesh):
    shards, ring = mesh.shape["hier"], mesh.shape["col"]

    def on_device(densities, hamiltonian, couplings, gamma, coeff, node_count):
        slots, _, rows, order = densities.shape
        f32, bf16 = jnp.float32, jnp.bfloat16
        vmem = pl.BlockSpec(memory_space=pltpu.VMEM)
        smem = pl.BlockSpec(memory_space=pltpu.SMEM)
        dma = pltpu.SemaphoreType.DMA
        wide = slots + 2 * DEPTH2
        block = (2, rows, order)
        return pl.pallas_call(
            functools.partial(kernel, shards, ring),
            out_shape=jax.ShapeDtypeStruct(densities.shape, f32),
            in_specs=[smem] * 3 + [pl.BlockSpec(memory_space=pltpu.HBM)] * 3,
            out_specs=vmem,
            scratch_shapes=[
                pltpu.VMEM((slots, *block), f32),
                pltpu.VMEM((order, order), f32),
                pltpu.VMEM((2, order, order), f32),
                pltpu.VMEM((2, DEPTH2, *block), f32),
                pltpu.VMEM((2, 2, DEPTH2, *block), f32),
                pltpu.VMEM((2, 2, DEPTH2, *block), f32),
                pltpu.VMEM((2, 2, DEPTH2, *block), f32),
                pltpu.VMEM((slots + 2 * REACH, *block), f32),
                pltpu.VMEM((wide, *block), f32),
                pltpu.VMEM((3 * order, order), bf16),
                pltpu.VMEM((3 * order, order), bf16),
                pltpu.VMEM((wide, 2 * rows, 3 * order), bf16),
                pltpu.VMEM((wide, 2 * rows, 3 * order), bf16),
                pltpu.VMEM((wide, *block), f32),
                pltpu.VMEM((wide, *block), f32),
                pltpu.VMEM((wide, *block), f32),
                pltpu.VMEM((2, slots, *block), f32),
                pltpu.VMEM((2, order, 9 * rows), bf16),
                pltpu.VMEM((2, order, 9 * rows), bf16),
                pltpu.VMEM((slots, *block), f32),
                pltpu.VMEM((slots, 9 * rows, 2 * order), bf16),
                pltpu.VMEM((slots, 9 * rows, 2 * order), bf16),
                pltpu.VMEM((slots, order, 2 * order), f32),
                pltpu.VMEM((slots, *block), f32),
                pltpu.VMEM((slots, *block), f32),
                pltpu.VMEM((ring, slots, rows, 2 * order), f32),
                pltpu.VMEM((ring, slots, rows, 2 * order), f32),
                dma((slots,)),
                dma((slots,)),
                dma((2, 2, 2)),
                dma((2, 2, 2)),
                dma((2, ring, slots)),
                dma((2, ring, slots)),
                dma((3,)),
            ],
            compiler_params=pltpu.CompilerParams(
                collective_id=0, has_side_effects=True, vmem_limit_bytes=67_043_328
            ),
        )(node_count, gamma, coeff, densities, hamiltonian, couplings)

    return jax.shard_map(
        on_device,
        mesh=mesh,
        in_specs=(P("hier", None, "col", None), P(), P(), P(), P(), P()),
        out_specs=P("hier", None, "col", None),
        check_vma=False,
    )
```
